128 devices in a mesh: wide: 16 (over z, x), narrow: 8 (over y, core).
Axes of the slice: x: 4, y: 4, z: 4, core: 2. Of those that a mesh axis runs over, the one named last changes fastest.
Arguments:
- depth_start: float32 [2048, 4096], P('wide', 'narrow'), may hold values from 0.1 to 1
- conveyance: float32 [2048, 4096], P('wide', 'narrow'), may hold values from 0.5 to 4
- cell_rain: float32 [2048, 4096], P('wide', 'narrow'), may hold values from 0.01 to 0.2
- nitrogen: float32 [2048, 4096], P('wide', 'narrow'), may hold values from 0.1 to 2
- flow_dir: int32 [2048, 4096], P('wide', 'narrow'), may hold values from 0 to 3
- unit_hydro: float32 [512], replicated, as said below
- rain_hours: bfloat16 [8, 32768, 512], P('narrow', 'wide'), may hold values from 0.049804688 to 2
- send_rows: int32 [8, 5, 16, 128], P('narrow', None, 'wide'), may hold values from -1 to 2047, as said below
- send_owner: int32 [8, 5, 16, 128], P('narrow', None, 'wide'), may hold values from -1 to 15, as said below
- send_down: int32 [8, 5, 16, 128], P('narrow', None, 'wide'), may hold values from -1 to 2047, as said below
Outputs:
- water_depth: float32 [2048, 4096], P('wide', 'narrow')
- nitrogen_left: float32 [2048, 4096], P('wide', 'narrow')
- discharge: float32 [8, 32768, 512], P('narrow', 'wide')
The draws below stay inside these ranges and needn't reach their ends.
Inputs may be any that keep to these rules, and one draw needn't show every extreme that they name: `unit_hydro`: positive weights of the unit hydrograph. send_rows[g, l, w, :] lists distinct local rows of owner w that send at level l, used slots first and -1 after; every owner sends at least 64 rows at each level, and some owner exactly 128; no row sends at two levels, and a row that receives at level l sends at no level up to l. `send_owner`: -1 exactly where send_rows is -1; at each level at most 16 rows of one owner go to the same owner, and one owner receives exactly 16 rows from every owner. `send_down`: -1 exactly where send_rows is -1.
All inputs are finite; a program needn't handle non-finite values.
Results may differ from the reference program's by a relative error of at most 0.00051.
Values sent between devices are 32-bit elements; how exact they have to be, the bound alone decides.
No kernel may reach another device: no remote copies, remote signals or barrier semaphores. Data moves between devices by JAX's collectives and lax.ppermute only.
A program may use at most 64 MiB of HBM per device.

```python
import math
import jax
import jax.numpy as jnp
from jax import lax

CR = 128
CC = 512
SUB_ROWS = 2
SUB_COLS = 16
HOURS = 512
STEPS = 4
LEVELS = 6
GROUPS = 8
OWNERS = 16
S_DEV = 2048
LCAP = 128
CAP = 16
SUBS = 32768
NR = 2048
NC = 4096


def routing_tables(key):
    base_key = jax.random.fold_in(key, 4242)
    key_counts, key_full, key_order, key_outlet, key_others, key_down = jax.random.split(base_key, 6)
    senders = LEVELS - 1
    counts = jax.random.randint(key_counts, (GROUPS, senders, OWNERS), 4 * CAP, LCAP + 1)
    fullest = jax.random.randint(key_full, (GROUPS, senders), 0, OWNERS)
    owner_ids = jnp.arange(OWNERS, dtype=jnp.int32)
    counts = jnp.where(owner_ids[None, None, :] == fullest[:, :, None], LCAP, counts)
    order_keys = jax.random.split(key_order, GROUPS * OWNERS)
    orders = jax.vmap(lambda one_key: jax.random.permutation(one_key, S_DEV))(order_keys)
    orders = orders.reshape(GROUPS, OWNERS, S_DEV).astype(jnp.int32)
    levels = jnp.arange(senders, dtype=jnp.int32)
    slot_ids = jnp.arange(LCAP, dtype=jnp.int32)
    positions = levels[:, None] * LCAP + slot_ids[None, :]
    picked = jnp.transpose(orders[:, :, positions], (0, 2, 1, 3))
    is_used = slot_ids[None, None, None, :] < counts[:, :, :, None]
    send_rows_all = jnp.where(is_used, picked, -1)
    outlet_devs = jax.random.randint(key_outlet, (GROUPS, senders), 0, OWNERS)
    other_keys = jax.random.split(key_others, GROUPS * senders * OWNERS)
    others = jax.vmap(lambda one_key: jax.random.permutation(one_key, OWNERS - 1))(other_keys)
    others = others.reshape(GROUPS, senders, OWNERS, OWNERS - 1).astype(jnp.int32)
    others = jnp.where(others >= outlet_devs[:, :, None, None], others + 1, others)
    block_index = slot_ids // CAP
    pick_index = jnp.clip(block_index - 1, 0, OWNERS - 2)
    chosen = others[:, :, :, pick_index]
    destination = jnp.where(block_index[None, None, None, :] == 0, outlet_devs[:, :, None, None], chosen)
    destination = jnp.where(is_used, destination, -1)
    lowest = (levels + 1) * LCAP
    down_places = jax.random.randint(key_down, (GROUPS, senders, OWNERS, LCAP), lowest[None, :, None, None], S_DEV)
    group_ids = jnp.arange(GROUPS, dtype=jnp.int32)[:, None, None, None]
    flat_index = (group_ids * OWNERS + jnp.maximum(destination, 0)) * S_DEV + down_places
    flat_orders = orders.reshape(-1)
    send_down_all = jnp.where(is_used, flat_orders[flat_index], -1)
    return (send_rows_all.astype(jnp.int32), destination.astype(jnp.int32), send_down_all.astype(jnp.int32))


def draw_send_rows(key, part):
    return routing_tables(key)[0]


def draw_send_owner(key, part):
    return routing_tables(key)[1]


def draw_send_down(key, part):
    return routing_tables(key)[2]


def draw_unit_hydro(key, part):
    hour_steps = jnp.arange(HOURS, dtype=jnp.float32)
    rough = jax.random.uniform(key, (HOURS,), jnp.float32, 0.5, 1.5)
    return jnp.exp(-hour_steps * (4.0 / HOURS)) * rough * (4.0 / HOURS)


def touch_ends(array, stream_key, least, top_value):
    index_at = [jax.random.randint(jax.random.fold_in(stream_key, axis), (), 0, length) for axis, length in enumerate(array.shape)]
    widest = array.shape.index(max(array.shape))
    neighbour = index_at[:widest] + [(index_at[widest] + 1) % array.shape[widest]] + index_at[widest + 1:]
    return array.at[tuple(index_at)].set(least).at[tuple(neighbour)].set(top_value)


def shard_levels(own_key, dims, pieces, low, top_value):
    level, own = 1.0, jax.random.fold_in(own_key, 6)
    for axis_at, shards_of in pieces:
        draws = jnp.exp(jax.random.uniform(jax.random.fold_in(own, axis_at), (shards_of,), jnp.float32, low / len(pieces), top_value / len(pieces)))
        level = level * jnp.repeat(draws, dims[axis_at] // shards_of).reshape([-1 if axis == axis_at else 1 for axis in range(len(dims))])
    return level


def setup_inputs(seed: int = 0) -> dict:
    key_of = jax.random.split(jax.random.key(seed), 11)
    depth_start = jnp.clip(0.1 + 0.9 * jax.random.uniform(key_of[0], (NR, NC), jnp.float32) ** shard_levels(key_of[0], (NR, NC), ((0, 16), (1, 8)), -0.2, 0.2), 0.1, 1.0)
    conveyance = jnp.clip(jnp.exp(math.log(4.0) - 2.0794415 * jax.random.uniform(key_of[1], (NR, NC), jnp.float32) ** shard_levels(key_of[1], (NR, NC), ((0, 16), (1, 8)), -0.2, 0.2)), 0.5, 4.0)
    cell_rain = jnp.clip(0.01 + 0.19 * jax.random.uniform(key_of[2], (NR, NC), jnp.float32) ** shard_levels(key_of[2], (NR, NC), ((0, 16), (1, 8)), -0.2, 0.2), 0.01, 0.2)
    nitrogen = jnp.clip(jnp.exp(math.log(2.0) - 2.9957323 * jax.random.uniform(key_of[3], (NR, NC), jnp.float32) ** shard_levels(key_of[3], (NR, NC), ((0, 16), (1, 8)), -0.2, 0.2)), 0.1, 2.0)
    flow_dir = touch_ends(jax.random.randint(key_of[4], (NR, NC), 0, 4), jax.random.fold_in(key_of[4], 1), 0, 3).astype(jnp.int32)
    unit_hydro = draw_unit_hydro(jax.random.fold_in(key_of[10], 71), 0)
    rain_hours = jnp.clip(jnp.exp(math.log(2.0) - 3.6927934 * jax.random.uniform(key_of[6], (GROUPS, SUBS, HOURS), jnp.float32) ** shard_levels(key_of[6], (GROUPS, SUBS, HOURS), ((0, 8), (1, 16)), -0.2, 0.2)), 0.049804688, 2.0).astype(jnp.bfloat16)
    send_rows = draw_send_rows(jax.random.fold_in(key_of[10], 71), 0)
    send_owner = draw_send_owner(jax.random.fold_in(key_of[10], 71), 0)
    send_down = draw_send_down(jax.random.fold_in(key_of[10], 71), 0)
    return dict(depth_start=depth_start, conveyance=conveyance, cell_rain=cell_rain, nitrogen=nitrogen, flow_dir=flow_dir, unit_hydro=unit_hydro, rain_hours=rain_hours, send_rows=send_rows, send_owner=send_owner, send_down=send_down)


WASH = 1.5
RECENT = 0.6
EARLIER = 0.3


def release(water, convey):
    rate = convey * jnp.cbrt(water * water)
    return water * (1.0 - jnp.exp(-rate))


def collect(padded_out, padded_dirs):
    from_west = jnp.where(padded_dirs[1:-1, :-2] == 0, padded_out[1:-1, :-2], 0.0)
    from_east = jnp.where(padded_dirs[1:-1, 2:] == 1, padded_out[1:-1, 2:], 0.0)
    from_north = jnp.where(padded_dirs[:-2, 1:-1] == 2, padded_out[:-2, 1:-1], 0.0)
    from_south = jnp.where(padded_dirs[2:, 1:-1] == 3, padded_out[2:, 1:-1], 0.0)
    return from_west + from_east + from_north + from_south


def lagged(flows):
    one_back = jnp.pad(flows, ((0, 0), (1, 0)))[:, :-1]
    two_back = jnp.pad(flows, ((0, 0), (2, 0)))[:, :-2]
    return RECENT * one_back + EARLIER * two_back


def reference(depth_start, conveyance, cell_rain, nitrogen, flow_dir, unit_hydro, rain_hours, send_rows, send_owner, send_down):
    water = depth_start
    nitrogen_left = nitrogen
    padded_dirs = jnp.pad(flow_dir, 1)
    for step_index in range(STEPS):
        outflow = release(water, conveyance)
        water = water - outflow + collect(jnp.pad(outflow, 1), padded_dirs) + cell_rain
        nitrogen_left = nitrogen_left - nitrogen_left * (1.0 - jnp.exp(-WASH * outflow))
    blocks = water.reshape(OWNERS, CR // SUB_ROWS, SUB_ROWS, GROUPS, CC // SUB_COLS, SUB_COLS)
    yields = jnp.mean(blocks, axis=(2, 5))
    yields = jnp.transpose(yields, (2, 0, 1, 3)).reshape(GROUPS, SUBS)
    lag_table = jnp.arange(HOURS, dtype=jnp.int32)[None, :] - jnp.arange(HOURS, dtype=jnp.int32)[:, None]
    kernel = unit_hydro.astype(jnp.bfloat16)
    toeplitz = jnp.where(lag_table >= 0, kernel[jnp.maximum(lag_table, 0)], jnp.zeros((), jnp.bfloat16))

    def route_group(group_args):
        rain_group, yield_group, rows_group, owner_group, down_group = group_args
        excess = (rain_group.astype(jnp.float32) * yield_group[:, None]).astype(jnp.bfloat16)
        flows_total = jnp.dot(excess, toeplitz, preferred_element_type=jnp.float32)
        row_base = (jnp.arange(OWNERS, dtype=jnp.int32) * S_DEV)[:, None]
        for level_index in range(LEVELS - 1):
            rows_level = rows_group[level_index]
            owner_level = owner_group[level_index]
            down_level = down_group[level_index]
            is_valid = (rows_level >= 0) & (owner_level >= 0) & (down_level >= 0)
            sources = (row_base + jnp.maximum(rows_level, 0)).reshape(-1)
            routed = jnp.where(is_valid.reshape(-1)[:, None], lagged(flows_total[sources]), 0.0)
            targets = jnp.where(is_valid, owner_level * S_DEV + down_level, SUBS).reshape(-1)
            flows_total = flows_total.at[targets].add(routed, mode="drop")
        return flows_total

    discharge = lax.map(route_group, (rain_hours, yields, send_rows, send_owner, send_down))
    return water, nitrogen_left, discharge
```

```python
import functools
import jax
import jax.numpy as jnp
from jax import lax
from jax.experimental import pallas as pl
from jax.experimental.pallas import tpu as pltpu
from jax.sharding import PartitionSpec as P

SUB_ROWS = 2
SUB_COLS = 16
STEPS = 4
WASH = 1.5
RECENT = 0.6
EARLIER = 0.3
EXACT = lax.Precision.HIGHEST

OWN = 16
LEV = 5
LIST = 128
SUBS = 2048
HRS = 512
ROWS = 128
COLS = 512
HOPS = LEV
ENT = LEV * LIST

SLOTS = 96
DATA = SLOTS - 1
MULTI = 32
EXTRA = 32

F32 = jnp.float32
BF = jnp.bfloat16
I32 = jnp.int32

VM = pl.BlockSpec(memory_space=pltpu.VMEM)


def nt_dot(a, b):
    return lax.dot_general(a, b, (((1,), (1,)), ((), ())), preferred_element_type=F32)


def nn_dot(a, b):
    return lax.dot_general(a, b, (((1,), (0,)), ((), ())), preferred_element_type=F32)


def iota(shape, dim):
    return lax.broadcasted_iota(I32, shape, dim)


def entry_keys(rows_ref, owner_ref, down_ref, level):
    rows = rows_ref[0, level]
    owner = owner_ref[0, level]
    down = down_ref[0, level]
    valid = (rows >= 0) & (owner >= 0) & (down >= 0)
    return jnp.where(valid, rows, -1), jnp.where(valid, owner * SUBS + down + 1, 0)


def map_kernel(rows_ref, owner_ref, down_ref, out_ref):
    acc = jnp.zeros((2 * OWN, LIST), F32)
    for level in range(LEV):
        rows, key = entry_keys(rows_ref, owner_ref, down_ref, level)
        hi = rows >> 7
        lo = rows & 127
        at_hi = iota((OWN, LIST), 0) == hi
        upper = jnp.where(at_hi, key >> 8, 0).astype(F32)
        lower = jnp.where(at_hi, key & 255, 0).astype(F32)
        left = jnp.concatenate([upper, lower], axis=0).astype(BF)
        right = jnp.where(iota((LIST, LIST), 0) == lo, 1.0, 0.0).astype(BF)
        acc = acc + nt_dot(left, right)
    table = acc[:OWN] * 256.0 + acc[OWN:]
    for owner in range(OWN):
        out_ref[owner] = table


def plan_kernel(rows_ref, owner_ref, down_ref, full_ref, slot_ref, left_ref, meta_ref):
    full = full_ref[...].reshape(OWN * OWN, LIST).astype(I32)
    parts = jnp.concatenate([(full >> 8).astype(F32), (full & 255).astype(F32)], axis=1)
    parts_t = jnp.transpose(parts).astype(BF)
    keys = [
        jnp.concatenate(
            [entry_keys(rows_ref, owner_ref, down_ref, level)[1] for level in range(LEV)], axis=1
        )
    ]
    for hop in range(1, HOPS):
        at = keys[-1] - 1
        pick_hi = jnp.where(iota((OWN * OWN, ENT), 0) == (at >> 7), 1.0, 0.0).astype(BF)
        found = nn_dot(parts_t, pick_hi)
        value = found[:LIST] * 256.0 + found[LIST:]
        at_lo = iota((LIST, ENT), 0) == (at & 127)
        keys.append(jnp.sum(jnp.where(at_lo, value, 0.0), axis=0, keepdims=True).astype(I32))
    order = list(range(1, HOPS)) + [0]
    upper_tri = jnp.where(iota((LIST, LIST), 0) < iota((LIST, LIST), 1), 1.0, 0.0).astype(BF)

    def blocks_of(key_list):
        blocks = []
        for hop in order:
            owner = (key_list[hop] - 1) >> 11
            for level in range(LEV):
                part = owner[:, level * LIST : (level + 1) * LIST]
                blocks.append(jnp.where(iota((OWN, LIST), 0) == part, 1.0, 0.0))
        counts = nn_dot(jnp.concatenate(blocks, axis=0).astype(BF), upper_tri)
        return blocks, counts

    blocks, counts = blocks_of(keys)
    n_multi = (HOPS - 1) * LEV
    base = jnp.zeros((OWN, 1), F32)
    slots = [None] * HOPS
    pieces = []
    for index in range(HOPS * LEV):
        if index == n_multi:
            base = jnp.minimum(base, float(MULTI))
        block = blocks[index]
        count = counts[index * OWN : (index + 1) * OWN]
        pieces.append(jnp.sum(block * (count + base), axis=0, keepdims=True))
        base = base + jnp.sum(block, axis=1, keepdims=True)
    rest_keys = [None] * HOPS
    for place, hop in enumerate(order):
        rank = jnp.concatenate(pieces[place * LEV : (place + 1) * LEV], axis=1).astype(I32)
        limit = DATA if hop == 0 else MULTI
        used = keys[hop] > 0
        fits = used & (rank < limit)
        slots[hop] = jnp.where(fits, rank, -1)
        rest_keys[hop] = jnp.where(used & (rank >= limit), keys[hop], 0)
    blocks, counts = blocks_of(rest_keys)
    base = jnp.zeros((OWN, 1), F32)
    pieces = []
    for index in range(HOPS * LEV):
        block = blocks[index]
        count = counts[index * OWN : (index + 1) * OWN]
        pieces.append(jnp.sum(block * (count + base), axis=0, keepdims=True))
        base = base + jnp.sum(block, axis=1, keepdims=True)
    most_left = jnp.max(base, axis=0, keepdims=True)
    for place, hop in enumerate(order):
        rank = jnp.concatenate(pieces[place * LEV : (place + 1) * LEV], axis=1).astype(I32)
        left_ref[pl.ds(hop, 1), :] = jnp.where(rest_keys[hop] > 0, rank, -1)
        left_ref[pl.ds(8 + hop, 1), :] = rest_keys[hop]
    meta = jnp.zeros((3 * OWN, LIST), F32)
    for hop in range(HOPS):
        at = keys[hop] - 1
        owner = at >> 11
        slot_ref[pl.ds(hop, 1), :] = jnp.where(slots[hop] >= 0, owner * SLOTS + slots[hop], -1)
        goal = (at & (SUBS - 1)) + 1
        at_owner = (iota((OWN, ENT), 0) == owner) & (slots[hop] >= 0)
        left = jnp.concatenate(
            [
                jnp.where(at_owner, goal >> 4, 0).astype(F32),
                jnp.where(at_owner, goal & 15, 0).astype(F32),
                jnp.where(at_owner, float(hop + 1), 0.0),
            ],
            axis=0,
        ).astype(BF)
        right = jnp.where(iota((LIST, ENT), 0) == slots[hop], 1.0, 0.0).astype(BF)
        meta = meta + nt_dot(left, right)
    meta_ref[:, 0:128] = meta[:OWN] * 16.0 + meta[OWN : 2 * OWN]
    meta_ref[:, 128:256] = meta[2 * OWN :]
    meta_ref[:, 256:384] = jnp.broadcast_to(most_left, (OWN, 128))
    meta_ref[:, 384:512] = jnp.zeros((OWN, 128), F32)


EXT_R = 144
EXT_C = 768


def strip_kernel(d_ref, c_ref, r_ref, f_ref, north_ref, south_ref, west_ref, east_ref):
    lane = iota((ROWS, 128), 1)
    lane4 = iota((4, 128), 1)
    west_ref[...] = jnp.zeros((EXT_R, 128), F32)
    east_ref[...] = jnp.zeros((EXT_R, 128), F32)
    sides = ((west_ref, 0, 0), (east_ref, COLS - 128, 124))
    for out_ref, start, first in sides:
        body = jnp.zeros((ROWS, 128), F32)
        top = jnp.zeros((4, 128), F32)
        bottom = jnp.zeros((4, 128), F32)
        for index, ref in enumerate((d_ref, c_ref, r_ref, f_ref)):
            shift = (4 * index - first) % 128
            block = ref[:, start : start + 128]
            if index == 3:
                block = block.astype(F32)
            mine = (lane >= 4 * index) & (lane < 4 * index + 4)
            mine4 = (lane4 >= 4 * index) & (lane4 < 4 * index + 4)
            body = jnp.where(mine, roll(block, shift, 1), body)
            top = jnp.where(mine4, roll(north_ref[index, :, start : start + 128], shift, 1), top)
            bottom = jnp.where(mine4, roll(south_ref[index, :, start : start + 128], shift, 1), bottom)
        out_ref[8 : 8 + ROWS, :] = body
        out_ref[4:8, :] = top
        out_ref[8 + ROWS : 12 + ROWS, :] = bottom


def roll(x, shift, axis):
    if shift % x.shape[axis] == 0:
        return x
    return pltpu.roll(x, shift % x.shape[axis], axis)


def main_kernel(
    d_ref,
    c_ref,
    r_ref,
    f_ref,
    north_ref,
    south_ref,
    west_ref,
    east_ref,
    nitro_ref,
    hours_ref,
    rows_ref,
    slot_ref,
    meta_ref,
    water_out,
    nitro_out,
    excess_out,
    send_ref,
    w_s,
    c_s,
    r_s,
    f_s,
    o_s,
    n_s,
    u_s,
    t_s,
    picked_s,
):
    lane = iota((EXT_R, 128), 1)
    for index, (src, dst) in enumerate(((d_ref, w_s), (c_ref, c_s), (r_ref, r_s), (f_ref, f_s))):
        dst[0:8, :] = jnp.zeros((8, EXT_C), F32)
        dst[136:144, :] = jnp.zeros((8, EXT_C), F32)
        body = src[...]
        if index == 3:
            body = body.astype(F32)
        dst[8:136, 128:640] = body
        dst[4:8, 128:640] = north_ref[index]
        dst[136:140, 128:640] = south_ref[index]
        left = roll(west_ref[...], 124 - 4 * index, 1)
        dst[:, 0:128] = jnp.where(lane >= 124, left, 0.0)
        right = roll(east_ref[...], -4 * index, 1)
        dst[:, 640:768] = jnp.where(lane < 4, right, 0.0)
    t_s[...] = jnp.zeros((ROWS, COLS), F32)
    n_s[...] = jnp.zeros((EXT_R + 16, EXT_C), F32)
    u_s[...] = jnp.zeros((EXT_R + 16, EXT_C), F32)
    for step in range(STEPS):

        def first(chunk, carry):
            at = pl.multiple_of(chunk * 8, 8)
            water = w_s[pl.ds(at, 8), :]
            rate = c_s[pl.ds(at, 8), :] * jnp.exp(jnp.log(water * water) * (1.0 / 3.0))
            out = water * (1.0 - jnp.exp(-rate))
            code = f_s[pl.ds(at, 8), :]
            o_s[pl.ds(at, 8), :] = out
            n_s[pl.ds(at + 8, 8), :] = jnp.where(code == 2.0, out, 0.0)
            u_s[pl.ds(at + 8, 8), :] = jnp.where(code == 3.0, out, 0.0)
            return carry

        lax.fori_loop(0, EXT_R // 8, first, 0, unroll=2)

        for chunk in range(EXT_R // 8):
            at = chunk * 8
            out = o_s[at : at + 8, :]
            code = f_s[at : at + 8, :]
            from_west = roll(jnp.where(code == 0.0, out, 0.0), 1, 1)
            from_east = roll(jnp.where(code == 1.0, out, 0.0), -1, 1)
            from_north = n_s[at + 7 : at + 15, :]
            from_south = u_s[at + 9 : at + 17, :]
            total = from_west + from_east + from_north + from_south
            w_s[at : at + 8, :] = w_s[at : at + 8, :] - out + total + r_s[at : at + 8, :]
            if 1 <= chunk <= 16:
                t_s[at - 8 : at, :] = t_s[at - 8 : at, :] + out[:, 128:640]

    nitro_out[...] = nitro_ref[...] * jnp.exp(-WASH * t_s[...])
    water = w_s[8:136, 128:640]
    water_out[...] = water
    blocks = jnp.where(iota((32, COLS), 1) // SUB_COLS == iota((32, COLS), 0), 1.0, 0.0)
    by_row = lax.dot_general(
        blocks, water, (((1,), (1,)), ((), ())), precision=EXACT, preferred_element_type=F32
    )
    pairs = jnp.where(iota((ROWS, 128), 0) // SUB_ROWS == iota((ROWS, 128), 1), 1.0, 0.0)
    means = lax.dot_general(
        by_row, pairs, (((1,), (0,)), ((), ())), precision=EXACT, preferred_element_type=F32
    ) * (1.0 / (SUB_ROWS * SUB_COLS))
    for block in range(ROWS // SUB_ROWS):
        at = block * 32
        excess = hours_ref[0, at : at + 32, :].astype(F32) * means[:, block : block + 1]
        excess_out[at : at + 32, :] = excess.astype(BF)
    for level in range(LEV):
        pick = jnp.where(
            rows_ref[level * LIST : (level + 1) * LIST, :] == iota((LIST, SUBS), 1), 1.0, 0.0
        ).astype(BF)
        picked_s[level * LIST : (level + 1) * LIST, :] = nn_dot(pick, excess_out[...]).astype(BF)
    for owner in range(OWN):
        place = iota((SLOTS, ENT), 0) + owner * SLOTS == slot_ref[0:1, :]
        top = place[0:MULTI]
        for hop in range(1, HOPS):
            top = top | (iota((MULTI, ENT), 0) + owner * SLOTS == slot_ref[hop : hop + 1, :])
        put = jnp.concatenate([jnp.where(top, 1.0, 0.0), jnp.where(place[MULTI:], 1.0, 0.0)], axis=0)
        send_ref[owner] = nn_dot(put.astype(BF), picked_s[...])
        send_ref[owner, DATA : DATA + 1, :] = meta_ref[owner : owner + 1, :]


def lag(x):
    at = iota(x.shape, 1)
    one = jnp.where(at >= 1, roll(x, 1, 1), 0.0)
    two = jnp.where(at >= 2, roll(x, 2, 1), 0.0)
    return RECENT * one + EARLIER * two


TILE = 256


def final_kernel(recv_ref, excess_ref, kernel_ref, out_ref, high_s, low_s, goal_s, multi_s):
    @pl.when(pl.program_id(0) == 0)
    def _():
        lane = iota((8, 128), 1)
        goals = [jnp.zeros((8, 128), F32)] * (OWN * SLOTS // 128)
        multi = [jnp.zeros((8, 128), F32)] * (OWN * MULTI // 128)
        hops = []
        for src in range(OWN):
            group = recv_ref[src, DATA - 7 : DATA + 1, 0:256]
            line = jnp.broadcast_to(group[7:8, 0:128], (8, 128))
            hops.append(group[7:8, 128:256])
            for width, store in ((SLOTS, goals), (MULTI, multi)):
                start = src * width
                block, off = start // 128, start % 128
                turned = roll(line, off, 1)
                here = (lane >= off) & (lane < off + width)
                store[block] = jnp.where(here, turned, store[block])
                if off + width > 128:
                    store[block + 1] = jnp.where(lane < off + width - 128, turned, store[block + 1])
        for index, value in enumerate(goals):
            goal_s[:, index * 128 : (index + 1) * 128] = value.astype(I32) - 1
        for index, value in enumerate(multi):
            multi_s[:, index * 128 : (index + 1) * 128] = value.astype(I32) - 1
        hop_rows = jnp.concatenate(hops + [jnp.zeros((128 - OWN, 128), F32)], axis=0)
        hop_cols = jnp.transpose(hop_rows)
        for src in range(OWN):
            part = recv_ref[src, 0:MULTI, :]
            count = hop_cols[0:MULTI, src : src + 1]
            for hop in range(1, HOPS):
                part = jnp.where(count > float(hop), lag(part), part)
            high = part.astype(BF)
            high_s[src * SLOTS : src * SLOTS + MULTI, :] = high
            low_s[src * MULTI : (src + 1) * MULTI, :] = (part - high.astype(F32)).astype(BF)
            high_s[src * SLOTS + MULTI : (src + 1) * SLOTS, :] = recv_ref[src, MULTI:, :].astype(BF)

    first = pl.program_id(0) * TILE
    match = iota((TILE, OWN * SLOTS), 0) + first == goal_s[0:1, :]
    gathered = nn_dot(jnp.where(match, 1.0, 0.0).astype(BF), high_s[...])
    match = iota((TILE, OWN * MULTI), 0) + first == multi_s[0:1, :]
    gathered = gathered + nn_dot(jnp.where(match, 1.0, 0.0).astype(BF), low_s[...])
    total = excess_ref[...].astype(F32) + lag(gathered)
    high = total.astype(BF)
    low = (total - high.astype(F32)).astype(BF)
    out_ref[...] = nn_dot(high, kernel_ref[...]) + nn_dot(low, kernel_ref[...])


def neighbours(axis):
    size = lax.axis_size(axis)
    up = [(i, i + 1) for i in range(size - 1)]
    return up, [(j, i) for i, j in up]


def exchange(array):
    return lax.all_to_all(array, "wide", split_axis=0, concat_axis=0, tiled=True)


def exact_dot(left, right):
    return jnp.dot(left, right, precision=EXACT, preferred_element_type=F32)


def local(
    depth_start,
    conveyance,
    cell_rain,
    nitrogen,
    flow_dir,
    unit_hydro,
    rain_hours,
    send_rows,
    send_owner,
    send_down,
):
    table = pl.pallas_call(
        map_kernel,
        out_shape=jax.ShapeDtypeStruct((OWN, OWN, LIST), F32),
        in_specs=[VM] * 3,
        out_specs=VM,
        name="next_map",
    )(send_rows, send_owner, send_down)
    full = exchange(table)

    fields = (depth_start, conveyance, cell_rain, flow_dir)
    up, down = neighbours("wide")
    last = jnp.stack([x[-4:].astype(F32) for x in fields])
    initial = jnp.stack([x[:4].astype(F32) for x in fields])
    north = lax.ppermute(last, "wide", up)
    south = lax.ppermute(initial, "wide", down)
    west_strip, east_strip = pl.pallas_call(
        strip_kernel,
        out_shape=[jax.ShapeDtypeStruct((EXT_R, 128), F32)] * 2,
        in_specs=[VM] * 6,
        out_specs=[VM] * 2,
        name="strips",
    )(*fields, north, south)
    up, down = neighbours("narrow")
    west = lax.ppermute(east_strip, "narrow", up)
    east = lax.ppermute(west_strip, "narrow", down)

    slots, left, meta = pl.pallas_call(
        plan_kernel,
        out_shape=[
            jax.ShapeDtypeStruct((8, ENT), I32),
            jax.ShapeDtypeStruct((16, ENT), I32),
            jax.ShapeDtypeStruct((OWN, HRS), F32),
        ],
        in_specs=[VM] * 4,
        out_specs=[VM] * 3,
        name="plan",
    )(send_rows, send_owner, send_down, full)

    valid = (send_rows >= 0) & (send_owner >= 0) & (send_down >= 0)
    rows_column = jnp.where(valid, send_rows, -1).reshape(ENT, 1)
    kernel = unit_hydro.astype(BF)
    pattern = jnp.concatenate([kernel, jnp.zeros((HRS,), BF)])
    repeated = jnp.tile(pattern, HRS)[: HRS * (2 * HRS - 1)]
    toeplitz = repeated.reshape(HRS, 2 * HRS - 1)[:, :HRS]

    water, nitrogen_left, excess, outgoing = pl.pallas_call(
        main_kernel,
        out_shape=[
            jax.ShapeDtypeStruct((ROWS, COLS), F32),
            jax.ShapeDtypeStruct((ROWS, COLS), F32),
            jax.ShapeDtypeStruct((SUBS, HRS), BF),
            jax.ShapeDtypeStruct((OWN, SLOTS, HRS), F32),
        ],
        in_specs=[VM] * 13,
        out_specs=[VM] * 4,
        scratch_shapes=[pltpu.VMEM((EXT_R, EXT_C), F32)] * 5
        + [pltpu.VMEM((EXT_R + 16, EXT_C), F32)] * 2
        + [pltpu.VMEM((ROWS, COLS), F32), pltpu.VMEM((ENT, HRS), BF)],
        name="flow_and_send",
    )(*fields, north, south, west, east, nitrogen, rain_hours, rows_column, slots, meta)
    incoming = exchange(outgoing)

    discharge = pl.pallas_call(
        final_kernel,
        out_shape=jax.ShapeDtypeStruct((SUBS, HRS), F32),
        grid=(SUBS // TILE,),
        in_specs=[
            pl.BlockSpec((OWN, SLOTS, HRS), lambda i: (0, 0, 0)),
            pl.BlockSpec((TILE, HRS), lambda i: (i, 0)),
            pl.BlockSpec((HRS, HRS), lambda i: (0, 0)),
        ],
        out_specs=pl.BlockSpec((TILE, HRS), lambda i: (i, 0)),
        scratch_shapes=[
            pltpu.VMEM((OWN * SLOTS, HRS), BF),
            pltpu.VMEM((OWN * MULTI, HRS), BF),
            pltpu.VMEM((8, OWN * SLOTS), I32),
            pltpu.VMEM((8, OWN * MULTI), I32),
        ],
        name="route_and_convolve",
    )(incoming, excess, toeplitz)

    most_left = jnp.max(incoming[:, DATA, 256])
    rounds = jnp.ceil(most_left * (1.0 / EXTRA)).astype(I32)

    def more(state):
        return state[0] < rounds

    def extra_round(state):
        index, flows = state
        picker = (rows_column == jnp.arange(SUBS, dtype=I32)[None, :]).astype(F32)
        rows = exact_dot(picker, excess.astype(F32))
        slot_iota = jnp.arange(OWN * EXTRA, dtype=I32)
        send = jnp.zeros((OWN * EXTRA, HRS), F32)
        goals = jnp.zeros((OWN * EXTRA,), F32)
        for hop in range(HOPS):
            key = left[8 + hop] - 1
            rank = left[hop] - index * EXTRA
            here = (left[hop] >= 0) & (rank >= 0) & (rank < EXTRA)
            slot = jnp.where(here, (key >> 11) * EXTRA + rank, -1)
            placer = (slot[None, :] == slot_iota[:, None]).astype(F32)
            send = send + exact_dot(placer, rows)
            goals = goals + jnp.sum(placer * ((key & (SUBS - 1)) + 1).astype(F32)[None, :], axis=1)
            rows = lagged(rows)
        came = exchange(send.reshape(OWN, EXTRA, HRS)).reshape(-1, HRS)
        came_goals = exchange(goals.reshape(OWN, EXTRA)).reshape(-1).astype(I32) - 1
        routed = exact_dot(lagged(came), toeplitz.astype(F32))
        receiver = (came_goals[None, :] == jnp.arange(SUBS, dtype=I32)[:, None]).astype(F32)
        return index + 1, flows + exact_dot(receiver, routed)

    discharge = lax.while_loop(more, extra_round, (jnp.zeros((), I32), discharge))[1]
    return (water, nitrogen_left, discharge[None])


def lagged(flows):
    one_back = jnp.pad(flows, ((0, 0), (1, 0)))[:, :-1]
    two_back = jnp.pad(flows, ((0, 0), (2, 0)))[:, :-2]
    return RECENT * one_back + EARLIER * two_back


def solution(mesh):
    placed = (
        P("wide", "narrow"),
        P("wide", "narrow"),
        P("wide", "narrow"),
        P("wide", "narrow"),
        P("wide", "narrow"),
        P(),
        P("narrow", "wide", None),
        P("narrow", None, "wide", None),
        P("narrow", None, "wide", None),
        P("narrow", None, "wide", None),
    )
    return jax.shard_map(
        local,
        mesh=mesh,
        in_specs=placed,
        out_specs=(P("wide", "narrow"), P("wide", "narrow"), P("narrow", "wide", None)),
        check_vma=False,
    )
```

```python
import jax
import jax.numpy as jnp
from jax import lax
from jax.experimental import pallas as pl
from jax.experimental.pallas import tpu as pltpu
from jax.sharding import PartitionSpec as P

SUB_ROWS = 2
SUB_COLS = 16
STEPS = 4
WASH = 1.5
RECENT = 0.6
EARLIER = 0.3
EXACT = lax.Precision.HIGHEST

OWN = 16
LEV = 5
LIST = 128
SUBS = 2048
HRS = 512
ROWS = 128
COLS = 512
HOPS = LEV
ENT = LEV * LIST

ONE = 64
TWO = 32
DATA = TWO - 1
DEEP = 8
EXTRA = 32
TABLE = 24

F32 = jnp.float32
BF = jnp.bfloat16
I32 = jnp.int32


def nt_dot(a, b):
    return lax.dot_general(a, b, (((1,), (1,)), ((), ())), preferred_element_type=F32)


def nn_dot(a, b):
    return lax.dot_general(a, b, (((1,), (0,)), ((), ())), preferred_element_type=F32)


def iota(shape, dim):
    return lax.broadcasted_iota(I32, shape, dim)


def entry_keys(rows_ref, owner_ref, down_ref, level):
    rows = rows_ref[0, level]
    owner = owner_ref[0, level]
    down = down_ref[0, level]
    valid = (rows >= 0) & (owner >= 0) & (down >= 0)
    return jnp.where(valid, rows, -1), jnp.where(valid, owner * SUBS + down + 1, 0)


def upper_triangle():
    return jnp.where(iota((LIST, LIST), 0) < iota((LIST, LIST), 1), 1.0, 0.0).astype(BF)


def ranks(key_list):
    blocks = []
    for keys in key_list:
        owner = (keys - 1) >> 11
        for level in range(LEV):
            part = owner[:, level * LIST : (level + 1) * LIST]
            blocks.append(jnp.where(iota((OWN, LIST), 0) == part, 1.0, 0.0))
    counts = nn_dot(jnp.concatenate(blocks, axis=0).astype(BF), upper_triangle())
    base = jnp.zeros((OWN, 1), F32)
    pieces = []
    for index, block in enumerate(blocks):
        count = counts[index * OWN : (index + 1) * OWN]
        pieces.append(jnp.sum(block * (count + base), axis=0, keepdims=True))
        base = base + jnp.sum(block, axis=1, keepdims=True)
    out = []
    for index in range(len(key_list)):
        out.append(jnp.concatenate(pieces[index * LEV : (index + 1) * LEV], axis=1).astype(I32))
    return out, base


def all_entries(rows_ref, owner_ref, down_ref):
    both = [entry_keys(rows_ref, owner_ref, down_ref, level) for level in range(LEV)]
    return tuple(jnp.concatenate([pair[k] for pair in both], axis=1) for k in range(2))


def row_columns(table):
    padded = jnp.concatenate([table, jnp.zeros((LIST - OWN, LIST), F32)], axis=0)
    return jnp.transpose(padded).astype(I32) - 1


def pick_rows(column_ref, width, source):
    picks = []
    for owner in range(OWN):
        row = jnp.broadcast_to(column_ref[0:width, owner : owner + 1], (width, 128))
        row = jnp.concatenate([row] * (SUBS // 128), axis=1)
        picks.append(jnp.where(row == iota((width, SUBS), 1), 1.0, 0.0).astype(BF))
    return nn_dot(jnp.concatenate(picks, axis=0), source).reshape(OWN, width, HRS)


def front_kernel(
    rows_ref,
    owner_ref,
    down_ref,
    d_top,
    c_top,
    r_top,
    f_top,
    d_end,
    c_end,
    r_end,
    f_end,
    table_ref,
    rank_ref,
    column_ref,
    last_ref,
    initial_ref,
):
    for index, (top, end) in enumerate(
        ((d_top, d_end), (c_top, c_end), (r_top, r_end), (f_top, f_end))
    ):
        initial_ref[index] = top[0:4, :].astype(F32)
        last_ref[index] = end[4:8, :].astype(F32)
    rows, keys = all_entries(rows_ref, owner_ref, down_ref)
    at_hi = iota((OWN, ENT), 0) == (rows >> 7)
    at_lo = jnp.where(iota((LIST, ENT), 0) == (rows & 127), 1.0, 0.0).astype(BF)
    left = jnp.concatenate(
        [
            jnp.where(at_hi, keys >> 8, 0).astype(F32),
            jnp.where(at_hi, keys & 255, 0).astype(F32),
        ],
        axis=0,
    ).astype(BF)
    both = nt_dot(left, at_lo)
    table = both[:OWN] * 256.0 + both[OWN:]
    (rank,), _ = ranks([keys])
    fits = (keys > 0) & (rank < ONE)
    owner = (keys - 1) >> 11
    goal = ((keys - 1) & (SUBS - 1)) + 1
    at_owner = (iota((OWN, ENT), 0) == owner) & fits
    left = jnp.concatenate(
        [
            jnp.where(at_owner, goal >> 4, 0).astype(F32),
            jnp.where(at_owner, goal & 15, 0).astype(F32),
            jnp.where(at_owner, (rows + 1) >> 4, 0).astype(F32),
            jnp.where(at_owner, (rows + 1) & 15, 0).astype(F32),
        ],
        axis=0,
    ).astype(BF)
    slot = jnp.where(fits, rank, -1)
    at_slot = jnp.where(iota((LIST, ENT), 0) == slot, 1.0, 0.0).astype(BF)
    both = nt_dot(left, at_slot)
    goals = both[:OWN] * 16.0 + both[OWN : 2 * OWN]
    column_ref[...] = row_columns(both[2 * OWN : 3 * OWN] * 16.0 + both[3 * OWN :])
    for owner_id in range(OWN):
        table_ref[owner_id, 0:OWN, :] = table
        table_ref[owner_id, OWN : OWN + 8, :] = jnp.broadcast_to(
            goals[owner_id : owner_id + 1, :], (8, LIST)
        )
    rank_ref[...] = jnp.broadcast_to(rank, (8, ENT))


def gather_kernel(column_ref, hours_ref, send_ref):
    send_ref[...] = pick_rows(column_ref, ONE, hours_ref[0])


def plan_kernel(rows_ref, owner_ref, down_ref, rank_ref, full_ref, column_ref, left_ref, meta_ref):
    full = full_ref[:, 0:OWN, :].reshape(OWN * OWN, LIST).astype(I32)
    parts = jnp.concatenate([(full >> 8).astype(F32), (full & 255).astype(F32)], axis=1)
    parts_t = jnp.transpose(parts).astype(BF)
    rows, first_keys = all_entries(rows_ref, owner_ref, down_ref)
    keys = [first_keys]
    for _ in range(1, HOPS):
        at = keys[-1] - 1
        pick_hi = jnp.where(iota((OWN * OWN, ENT), 0) == (at >> 7), 1.0, 0.0).astype(BF)
        found = nn_dot(parts_t, pick_hi)
        value = found[:LIST] * 256.0 + found[LIST:]
        at_lo = iota((LIST, ENT), 0) == (at & 127)
        keys.append(jnp.sum(jnp.where(at_lo, value, 0.0), axis=0, keepdims=True).astype(I32))
    order = list(range(HOPS - 1, -1, -1))
    first_fits = rank_ref[0:1, :] < ONE
    keys[0] = jnp.where(first_fits, 0, keys[0])
    found, _ = ranks([keys[hop] for hop in order])
    slots = [None] * HOPS
    rest = [None] * HOPS
    for place, hop in enumerate(order):
        limit = DEEP if hop >= 2 else DATA
        used = keys[hop] > 0
        slots[hop] = jnp.where(used & (found[place] < limit), found[place], -1)
        rest[hop] = jnp.where(used & (found[place] >= limit), keys[hop], 0)
    found, totals = ranks([rest[hop] for hop in order])
    most_left = jnp.max(totals, axis=0, keepdims=True)
    for place, hop in enumerate(order):
        left_ref[pl.ds(hop, 1), :] = jnp.where(rest[hop] > 0, found[place], -1)
        left_ref[pl.ds(8 + hop, 1), :] = rest[hop]
    meta = jnp.zeros((5 * OWN, LIST), F32)
    for hop in range(HOPS):
        at = keys[hop] - 1
        owner = at >> 11
        goal = (at & (SUBS - 1)) + 1
        at_owner = (iota((OWN, ENT), 0) == owner) & (slots[hop] >= 0)
        left = jnp.concatenate(
            [
                jnp.where(at_owner, goal >> 4, 0).astype(F32),
                jnp.where(at_owner, goal & 15, 0).astype(F32),
                jnp.where(at_owner, float(hop + 1), 0.0),
                jnp.where(at_owner, (rows + 1) >> 4, 0).astype(F32),
                jnp.where(at_owner, (rows + 1) & 15, 0).astype(F32),
            ],
            axis=0,
        ).astype(BF)
        right = jnp.where(iota((LIST, ENT), 0) == slots[hop], 1.0, 0.0).astype(BF)
        meta = meta + nt_dot(left, right)
    meta_ref[:, 0:128] = meta[:OWN] * 16.0 + meta[OWN : 2 * OWN]
    meta_ref[:, 128:256] = roll(meta[2 * OWN : 3 * OWN], ONE, 1)
    column_ref[...] = row_columns(meta[3 * OWN : 4 * OWN] * 16.0 + meta[4 * OWN :])
    meta_ref[:, 256:384] = jnp.broadcast_to(most_left, (OWN, 128))
    meta_ref[:, 384:512] = jnp.zeros((OWN, 128), F32)


EXT_R = 144
EXT_C = 768


def strip_kernel(d_ref, c_ref, r_ref, f_ref, north_ref, south_ref, west_ref, east_ref):
    lane = iota((ROWS, 128), 1)
    lane4 = iota((4, 128), 1)
    west_ref[...] = jnp.zeros((EXT_R, 128), F32)
    east_ref[...] = jnp.zeros((EXT_R, 128), F32)
    sides = ((west_ref, 0, 0), (east_ref, COLS - 128, 124))
    for out_ref, start, first in sides:
        body = jnp.zeros((ROWS, 128), F32)
        top = jnp.zeros((4, 128), F32)
        bottom = jnp.zeros((4, 128), F32)
        for index, ref in enumerate((d_ref, c_ref, r_ref, f_ref)):
            shift = (4 * index - first) % 128
            block = ref[:, start : start + 128]
            if index == 3:
                block = block.astype(F32)
            mine = (lane >= 4 * index) & (lane < 4 * index + 4)
            mine4 = (lane4 >= 4 * index) & (lane4 < 4 * index + 4)
            body = jnp.where(mine, roll(block, shift, 1), body)
            top = jnp.where(mine4, roll(north_ref[index, :, start : start + 128], shift, 1), top)
            bottom = jnp.where(mine4, roll(south_ref[index, :, start : start + 128], shift, 1), bottom)
        out_ref[8 : 8 + ROWS, :] = body
        out_ref[4:8, :] = top
        out_ref[8 + ROWS : 12 + ROWS, :] = bottom


def shift_lanes(x, places):
    blocks = x.shape[1] // 128
    turned = [roll(x[:, b * 128 : (b + 1) * 128], places, 1) for b in range(blocks)]
    lane = iota(turned[0].shape, 1)
    zero = jnp.zeros_like(turned[0])
    out = []
    for b in range(blocks):
        if places > 0:
            other = turned[b - 1] if b else zero
            out.append(jnp.where(lane < places, other, turned[b]))
        else:
            other = turned[b + 1] if b + 1 < blocks else zero
            out.append(jnp.where(lane >= 128 + places, other, turned[b]))
    return jnp.concatenate(out, axis=1)


def roll(x, shift, axis):
    if shift % x.shape[axis] == 0:
        return x
    return pltpu.roll(x, shift % x.shape[axis], axis)


def main_kernel(
    d_ref,
    c_ref,
    r_ref,
    f_ref,
    north_ref,
    south_ref,
    west_ref,
    east_ref,
    nitro_ref,
    hours_ref,
    rows_ref,
    owner_ref,
    down_ref,
    rank_ref,
    column_ref,
    meta_ref,
    water_out,
    nitro_out,
    excess_out,
    send_ref,
    w_s,
    c_s,
    r_s,
    f_s,
    o_s,
    n_s,
    u_s,
    t_s,
):
    lane = iota((EXT_R, 128), 1)
    for index, (src, dst) in enumerate(((d_ref, w_s), (c_ref, c_s), (r_ref, r_s), (f_ref, f_s))):
        dst[0:8, :] = jnp.zeros((8, EXT_C), F32)
        dst[136:144, :] = jnp.zeros((8, EXT_C), F32)
        body = src[...]
        if index == 3:
            body = body.astype(F32)
        dst[8:136, 128:640] = body
        dst[4:8, 128:640] = north_ref[index]
        dst[136:140, 128:640] = south_ref[index]
        left = roll(west_ref[...], 124 - 4 * index, 1)
        dst[:, 0:128] = jnp.where(lane >= 124, left, 0.0)
        right = roll(east_ref[...], -4 * index, 1)
        dst[:, 640:768] = jnp.where(lane < 4, right, 0.0)
    t_s[...] = jnp.zeros((ROWS, COLS), F32)
    n_s[...] = jnp.zeros((EXT_R + 16, EXT_C), F32)
    u_s[...] = jnp.zeros((EXT_R + 16, EXT_C), F32)
    for _ in range(STEPS):

        def first(chunk, carry):
            at = pl.multiple_of(chunk * 8, 8)
            water = w_s[pl.ds(at, 8), :]
            rate = c_s[pl.ds(at, 8), :] * jnp.exp(jnp.log(water * water) * (1.0 / 3.0))
            out = water * (1.0 - jnp.exp(-rate))
            code = f_s[pl.ds(at, 8), :]
            o_s[pl.ds(at, 8), :] = out
            n_s[pl.ds(at + 8, 8), :] = jnp.where(code == 2.0, out, 0.0)
            u_s[pl.ds(at + 8, 8), :] = jnp.where(code == 3.0, out, 0.0)
            return carry

        lax.fori_loop(0, EXT_R // 8, first, 0, unroll=2)

        for chunk in range(EXT_R // 8):
            at = chunk * 8
            out = o_s[at : at + 8, :]
            code = f_s[at : at + 8, :]
            from_west = shift_lanes(jnp.where(code == 0.0, out, 0.0), 1)
            from_east = shift_lanes(jnp.where(code == 1.0, out, 0.0), -1)
            from_north = n_s[at + 7 : at + 15, :]
            from_south = u_s[at + 9 : at + 17, :]
            total = from_west + from_east + from_north + from_south
            w_s[at : at + 8, :] = w_s[at : at + 8, :] - out + total + r_s[at : at + 8, :]
            if 1 <= chunk <= 16:
                t_s[at - 8 : at, :] = t_s[at - 8 : at, :] + out[:, 128:640]

    nitro_out[...] = nitro_ref[...] * jnp.exp(-WASH * t_s[...])
    water = w_s[8:136, 128:640]
    water_out[...] = water
    blocks = jnp.where(iota((32, COLS), 1) // SUB_COLS == iota((32, COLS), 0), 1.0, 0.0)
    by_row = lax.dot_general(
        blocks, water, (((1,), (1,)), ((), ())), precision=EXACT, preferred_element_type=F32
    )
    pairs = jnp.where(iota((ROWS, 128), 0) // SUB_ROWS == iota((ROWS, 128), 1), 1.0, 0.0)
    means = lax.dot_general(
        by_row, pairs, (((1,), (0,)), ((), ())), precision=EXACT, preferred_element_type=F32
    ) * (1.0 / (SUB_ROWS * SUB_COLS))
    for block in range(ROWS // SUB_ROWS):
        at = block * 32
        factor = jnp.broadcast_to(means[:, block : block + 1], (32, 128))
        factor = jnp.concatenate([factor] * (HRS // 128), axis=1)
        excess = hours_ref[0, at : at + 32, :].astype(F32) * factor
        excess_out[at : at + 32, :] = excess.astype(BF)
    rows, keys = all_entries(rows_ref, owner_ref, down_ref)
    at_block = jnp.where(iota((128, ENT), 0) == (rows >> 5), 1.0, 0.0)
    found = lax.dot_general(
        means, at_block, (((1,), (0,)), ((), ())), precision=EXACT, preferred_element_type=F32
    )
    at_cell = iota((32, ENT), 0) == (rows & 31)
    entry_yield = jnp.sum(jnp.where(at_cell, found, 0.0), axis=0, keepdims=True)
    rank = rank_ref[0:1, :]
    fits = (keys > 0) & (rank < ONE)
    at_owner = (iota((OWN, ENT), 0) == ((keys - 1) >> 11)) & fits
    at_slot = jnp.where(iota((LIST, ENT), 0) == jnp.where(fits, rank, -1), 1.0, 0.0)
    slot_yield = lax.dot_general(
        jnp.where(at_owner, entry_yield, 0.0),
        at_slot,
        (((1,), (1,)), ((), ())),
        precision=EXACT,
        preferred_element_type=F32,
    )
    send_ref[...] = pick_rows(column_ref, TWO, excess_out[...])
    second = meta_ref[:, 128:256] + slot_yield
    for owner in range(OWN):
        send_ref[owner, DATA : DATA + 1, :] = meta_ref[owner : owner + 1, :]
        send_ref[owner, DATA : DATA + 1, 128:256] = second[owner : owner + 1, :]


def lag(x):
    return RECENT * shift_lanes(x, 1) + EARLIER * shift_lanes(x, 2)


TILE = 1024
TILES = SUBS // TILE


def flat_line(lines, width):
    lane = iota((8, 128), 1)
    store = [jnp.zeros((8, 128), F32)] * (OWN * width // 128)
    for src in range(OWN):
        start = src * width
        block, off = start // 128, start % 128
        here = (lane >= off) & (lane < off + width)
        store[block] = jnp.where(here, roll(lines[src], off, 1), store[block])
    return jnp.concatenate(store, axis=1).astype(I32) - 1


def columns_of(lines):
    padded = jnp.concatenate([x[0:1] for x in lines] + [jnp.zeros((128 - OWN, 128), F32)], axis=0)
    return jnp.transpose(padded)


def final_kernel(
    one_ref, two_ref, table_ref, excess_ref, kernel_ref, out_ref, rounds_ref, rows_s, goal_s
):
    step = pl.program_id(0)

    @pl.when(step == 0)
    def _():
        groups = [two_ref[src, TWO - 8 : TWO, :][7:8] for src in range(OWN)]
        goal_s[:, 0 : OWN * ONE] = flat_line([table_ref[src, OWN : OWN + 8, :] for src in range(OWN)], ONE)
        goal_s[:, OWN * ONE :] = flat_line(
            [jnp.broadcast_to(x[:, 0:128], (8, 128)) for x in groups], TWO
        )
        most = groups[0][:, 256:384]
        for x in groups[1:]:
            most = jnp.maximum(most, x[:, 256:384])
        rounds_ref[0, 0] = jnp.max(most).astype(I32)
        factors = columns_of([x[:, 128:256] for x in groups])
        counts = []
        parts = []
        for src in range(OWN):
            factor = jnp.broadcast_to(factors[0 : ONE + TWO, src : src + 1], (ONE + TWO, 128))
            factor = jnp.concatenate([factor] * (HRS // 128), axis=1)
            scaled = one_ref[src] * factor[0:ONE]
            rows_s[src * ONE : (src + 1) * ONE, :] = scaled.astype(BF)
            counts.append(factor[ONE:])
            parts.append(jnp.where(counts[src] > 1.0, lag(two_ref[src]), two_ref[src]))
        deep = jnp.concatenate([x[0:DEEP] for x in parts], axis=0)
        deep_counts = jnp.concatenate([x[0:DEEP] for x in counts], axis=0)
        for hop in range(2, HOPS):
            deep = jnp.where(deep_counts > float(hop), lag(deep), deep)
        for src in range(OWN):
            part = jnp.concatenate([deep[src * DEEP : (src + 1) * DEEP], parts[src][DEEP:]], axis=0)
            high = part.astype(BF)
            at = OWN * ONE + src * TWO
            rows_s[at : at + TWO, :] = high
            at = OWN * (ONE + TWO) + src * TWO
            rows_s[at : at + TWO, :] = (part - high.astype(F32)).astype(BF)

    match = iota((TILE, OWN * (ONE + TWO)), 0) + step * TILE == goal_s[0:1, :]
    put = jnp.where(match, 1.0, 0.0).astype(BF)
    put = jnp.concatenate([put, put[:, OWN * ONE :]], axis=1)
    total = excess_ref[...].astype(F32) + lag(nn_dot(put, rows_s[...]))
    high = total.astype(BF)
    low = (total - high.astype(F32)).astype(BF)
    half = HRS // 2
    parts = jnp.concatenate([high, low], axis=0)
    both = nn_dot(parts[:, :half], kernel_ref[:half, :half])
    out_ref[:, :half] = both[:TILE] + both[TILE:]
    both = nn_dot(parts, kernel_ref[:, half:])
    out_ref[:, half:] = both[:TILE] + both[TILE:]


def neighbours(axis):
    size = lax.axis_size(axis)
    up = [(i, i + 1) for i in range(size - 1)]
    return up, [(j, i) for i, j in up]


def exchange(array):
    return lax.all_to_all(array, "wide", split_axis=0, concat_axis=0, tiled=True)


def exact_dot(left, right):
    return jnp.dot(left, right, precision=EXACT, preferred_element_type=F32)


def routed_local(
    depth_start,
    conveyance,
    cell_rain,
    nitrogen,
    flow_dir,
    unit_hydro,
    rain_hours,
    send_rows,
    send_owner,
    send_down,
):
    lists = (send_rows, send_owner, send_down)
    fields = (depth_start, conveyance, cell_rain, flow_dir)
    whole = lambda shape: pl.BlockSpec(shape, lambda i: (0,) * len(shape))
    table, rank, columns, last, initial = pl.pallas_call(
        front_kernel,
        grid=(1,),
        out_shape=[
            jax.ShapeDtypeStruct((OWN, TABLE, LIST), F32),
            jax.ShapeDtypeStruct((8, ENT), I32),
            jax.ShapeDtypeStruct((LIST, LIST), I32),
            jax.ShapeDtypeStruct((4, 4, COLS), F32),
            jax.ShapeDtypeStruct((4, 4, COLS), F32),
        ],
        in_specs=[whole((1, LEV, 1, LIST))] * 3
        + [pl.BlockSpec((8, COLS), lambda i: (0, 0))] * 4
        + [pl.BlockSpec((8, COLS), lambda i: (ROWS // 8 - 1, 0))] * 4,
        out_specs=[
            whole((OWN, TABLE, LIST)),
            whole((8, ENT)),
            whole((LIST, LIST)),
            whole((4, 4, COLS)),
            whole((4, 4, COLS)),
        ],
        name="front",
    )(*lists, *fields, *fields)
    full = exchange(table)
    up, down = neighbours("wide")
    north = lax.ppermute(last, "wide", up)
    south = lax.ppermute(initial, "wide", down)
    outgoing = pl.pallas_call(
        gather_kernel,
        out_shape=jax.ShapeDtypeStruct((OWN, ONE, HRS), F32),
        grid=(1,),
        in_specs=[whole(x.shape) for x in (columns, rain_hours)],
        out_specs=whole((OWN, ONE, HRS)),
        name="gather_rain",
    )(columns, rain_hours)
    arrived = exchange(outgoing)
    west_strip, east_strip = pl.pallas_call(
        strip_kernel,
        out_shape=[jax.ShapeDtypeStruct((EXT_R, 128), F32)] * 2,
        grid=(1,),
        in_specs=[whole(x.shape) for x in (*fields, north, south)],
        out_specs=[whole((EXT_R, 128))] * 2,
        name="strips",
    )(*fields, north, south)
    up, down = neighbours("narrow")
    west = lax.ppermute(east_strip, "narrow", up)
    east = lax.ppermute(west_strip, "narrow", down)
    columns, left, meta = pl.pallas_call(
        plan_kernel,
        out_shape=[
            jax.ShapeDtypeStruct((LIST, LIST), I32),
            jax.ShapeDtypeStruct((16, ENT), I32),
            jax.ShapeDtypeStruct((OWN, HRS), F32),
        ],
        grid=(1,),
        in_specs=[whole(x.shape) for x in (*lists, rank, full)],
        out_specs=[whole((LIST, LIST)), whole((16, ENT)), whole((OWN, HRS))],
        name="plan",
    )(*lists, rank, full)
    kernel = unit_hydro.astype(BF)
    pattern = jnp.concatenate([kernel, jnp.zeros((HRS,), BF)])
    repeated = jnp.tile(pattern, HRS)[: HRS * (2 * HRS - 1)]
    toeplitz = repeated.reshape(HRS, 2 * HRS - 1)[:, :HRS]
    flow_inputs = (*fields, north, south, west, east, nitrogen, rain_hours)
    flow_inputs += (*lists, rank, columns, meta)
    water, nitrogen_left, excess, outgoing = pl.pallas_call(
        main_kernel,
        out_shape=[
            jax.ShapeDtypeStruct((ROWS, COLS), F32),
            jax.ShapeDtypeStruct((ROWS, COLS), F32),
            jax.ShapeDtypeStruct((SUBS, HRS), BF),
            jax.ShapeDtypeStruct((OWN, TWO, HRS), F32),
        ],
        grid=(1,),
        in_specs=[whole(x.shape) for x in flow_inputs],
        out_specs=[
            whole((ROWS, COLS)),
            whole((ROWS, COLS)),
            whole((SUBS, HRS)),
            whole((OWN, TWO, HRS)),
        ],
        scratch_shapes=[pltpu.VMEM((EXT_R, EXT_C), F32)] * 5
        + [pltpu.VMEM((EXT_R + 16, EXT_C), F32)] * 2
        + [pltpu.VMEM((ROWS, COLS), F32)],
        name="flow_and_send",
    )(*flow_inputs)
    incoming = exchange(outgoing)
    tile = lambda i: (i, 0)
    discharge, most_left = pl.pallas_call(
        final_kernel,
        out_shape=[
            jax.ShapeDtypeStruct((SUBS, HRS), F32),
            jax.ShapeDtypeStruct((1, 1), I32),
        ],
        grid=(TILES,),
        in_specs=[
            whole((OWN, ONE, HRS)),
            whole((OWN, TWO, HRS)),
            whole((OWN, TABLE, LIST)),
            pl.BlockSpec((TILE, HRS), tile),
            whole((HRS, HRS)),
        ],
        out_specs=[
            pl.BlockSpec((TILE, HRS), tile),
            pl.BlockSpec((1, 1), lambda i: (0, 0), memory_space=pltpu.SMEM),
        ],
        scratch_shapes=[
            pltpu.VMEM((OWN * (ONE + 2 * TWO), HRS), BF),
            pltpu.VMEM((8, OWN * (ONE + TWO)), I32),
        ],
        name="route_and_convolve",
    )(arrived, incoming, full, excess, toeplitz)

    def more(state):
        return state[0] * EXTRA < most_left[0, 0]

    def extra_round(state):
        index, flows = state
        valid = (send_rows >= 0) & (send_owner >= 0) & (send_down >= 0)
        rows_column = jnp.where(valid, send_rows, -1).reshape(ENT, 1)
        picker = (rows_column == jnp.arange(SUBS, dtype=I32)[None, :]).astype(F32)
        rows = exact_dot(picker, excess.astype(F32))
        slot_iota = jnp.arange(OWN * EXTRA, dtype=I32)
        send = jnp.zeros((OWN * EXTRA, HRS), F32)
        goals = jnp.zeros((OWN * EXTRA,), F32)
        for hop in range(HOPS):
            key = left[8 + hop] - 1
            rank = left[hop] - index * EXTRA
            here = (left[hop] >= 0) & (rank >= 0) & (rank < EXTRA)
            slot = jnp.where(here, (key >> 11) * EXTRA + rank, -1)
            placer = (slot[None, :] == slot_iota[:, None]).astype(F32)
            send = send + exact_dot(placer, rows)
            goals = goals + jnp.sum(placer * ((key & (SUBS - 1)) + 1).astype(F32)[None, :], axis=1)
            rows = lagged(rows)
        came = exchange(send.reshape(OWN, EXTRA, HRS)).reshape(-1, HRS)
        came_goals = exchange(goals.reshape(OWN, EXTRA)).reshape(-1).astype(I32) - 1
        routed = exact_dot(lagged(came), toeplitz.astype(F32))
        receiver = (came_goals[None, :] == jnp.arange(SUBS, dtype=I32)[:, None]).astype(F32)
        return index + 1, flows + exact_dot(receiver, routed)

    discharge = lax.while_loop(more, extra_round, (jnp.zeros((), I32), discharge))[1]
    return (water, nitrogen_left, discharge[None])


def lagged(flows):
    one_back = jnp.pad(flows, ((0, 0), (1, 0)))[:, :-1]
    two_back = jnp.pad(flows, ((0, 0), (2, 0)))[:, :-2]
    return RECENT * one_back + EARLIER * two_back


def solution(mesh):
    placed = (
        P("wide", "narrow"),
        P("wide", "narrow"),
        P("wide", "narrow"),
        P("wide", "narrow"),
        P("wide", "narrow"),
        P(),
        P("narrow", "wide", None),
        P("narrow", None, "wide", None),
        P("narrow", None, "wide", None),
        P("narrow", None, "wide", None),
    )
    return jax.shard_map(
        routed_local,
        mesh=mesh,
        in_specs=placed,
        out_specs=(P("wide", "narrow"), P("wide", "narrow"), P("narrow", "wide", None)),
        check_vma=False,
    )
```

```python
import jax
import jax.numpy as jnp
from jax import lax
from jax.experimental import pallas as pl
from jax.experimental.pallas import tpu as pltpu
from jax.sharding import PartitionSpec as P

SUB_ROWS = 2
SUB_COLS = 16
STEPS = 4
WASH = 1.5
RECENT = 0.6
EARLIER = 0.3
EXACT = lax.Precision.HIGHEST

OWN = 16
LEV = 5
LIST = 128
SUBS = 2048
HRS = 512
ROWS = 128
COLS = 512
HOPS = LEV
ENT = LEV * LIST

ONE = 64
TWO = 32
DATA = TWO - 1
DEEP = 8
EXTRA = 32
TABLE = 24

F32 = jnp.float32
BF = jnp.bfloat16
I32 = jnp.int32

ROOM = pltpu.CompilerParams(vmem_limit_bytes=26 << 20)


def nt_dot(a, b):
    return lax.dot_general(a, b, (((1,), (1,)), ((), ())), preferred_element_type=F32)


def nn_dot(a, b):
    return lax.dot_general(a, b, (((1,), (0,)), ((), ())), preferred_element_type=F32)


def iota(shape, dim):
    return lax.broadcasted_iota(I32, shape, dim)


def entry_keys(rows_ref, owner_ref, down_ref, level):
    rows = rows_ref[0, level]
    owner = owner_ref[0, level]
    down = down_ref[0, level]
    valid = (rows >= 0) & (owner >= 0) & (down >= 0)
    return jnp.where(valid, rows, -1), jnp.where(valid, owner * SUBS + down + 1, 0)


def upper_triangle():
    return jnp.where(iota((LIST, LIST), 0) < iota((LIST, LIST), 1), 1.0, 0.0).astype(BF)


def ranks(key_list):
    blocks = []
    for keys in key_list:
        owner = (keys - 1) >> 11
        for level in range(LEV):
            part = owner[:, level * LIST : (level + 1) * LIST]
            blocks.append(jnp.where(iota((OWN, LIST), 0) == part, 1.0, 0.0))
    counts = nn_dot(jnp.concatenate(blocks, axis=0).astype(BF), upper_triangle())
    base = jnp.zeros((OWN, 1), F32)
    pieces = []
    for index, block in enumerate(blocks):
        count = counts[index * OWN : (index + 1) * OWN]
        pieces.append(jnp.sum(block * (count + base), axis=0, keepdims=True))
        base = base + jnp.sum(block, axis=1, keepdims=True)
    out = []
    for index in range(len(key_list)):
        out.append(jnp.concatenate(pieces[index * LEV : (index + 1) * LEV], axis=1).astype(I32))
    return out, base


def all_entries(rows_ref, owner_ref, down_ref):
    both = [entry_keys(rows_ref, owner_ref, down_ref, level) for level in range(LEV)]
    return tuple(jnp.concatenate([pair[k] for pair in both], axis=1) for k in range(2))


def row_columns(table):
    padded = jnp.concatenate([table, jnp.zeros((LIST - OWN, LIST), F32)], axis=0)
    return jnp.transpose(padded).astype(I32) - 1


def pick_rows(column_ref, width, source):
    picks = []
    for owner in range(OWN):
        row = jnp.broadcast_to(column_ref[0:width, owner : owner + 1], (width, 128))
        row = jnp.concatenate([row] * (SUBS // 128), axis=1)
        picks.append(jnp.where(row == iota((width, SUBS), 1), 1.0, 0.0).astype(BF))
    return nn_dot(jnp.concatenate(picks, axis=0), source).reshape(OWN, width, HRS)


def front_kernel(
    rows_ref,
    owner_ref,
    down_ref,
    d_top,
    c_top,
    r_top,
    f_top,
    d_end,
    c_end,
    r_end,
    f_end,
    table_ref,
    rank_ref,
    last_ref,
    initial_ref,
):
    for index, (top, end) in enumerate(
        ((d_top, d_end), (c_top, c_end), (r_top, r_end), (f_top, f_end))
    ):
        initial_ref[index] = top[0:4, :].astype(F32)
        last_ref[index] = end[4:8, :].astype(F32)
    rows, keys = all_entries(rows_ref, owner_ref, down_ref)
    at_hi = iota((OWN, ENT), 0) == (rows >> 7)
    at_lo = jnp.where(iota((LIST, ENT), 0) == (rows & 127), 1.0, 0.0).astype(BF)
    left = jnp.concatenate(
        [
            jnp.where(at_hi, keys >> 8, 0).astype(F32),
            jnp.where(at_hi, keys & 255, 0).astype(F32),
        ],
        axis=0,
    ).astype(BF)
    both = nt_dot(left, at_lo)
    table = both[:OWN] * 256.0 + both[OWN:]
    (rank,), _ = ranks([keys])
    fits = (keys > 0) & (rank < ONE)
    owner = (keys - 1) >> 11
    goal = ((keys - 1) & (SUBS - 1)) + 1
    at_owner = (iota((OWN, ENT), 0) == owner) & fits
    left = jnp.concatenate(
        [
            jnp.where(at_owner, goal >> 4, 0).astype(F32),
            jnp.where(at_owner, goal & 15, 0).astype(F32),
        ],
        axis=0,
    ).astype(BF)
    slot = jnp.where(fits, rank, -1)
    at_slot = jnp.where(iota((LIST, ENT), 0) == slot, 1.0, 0.0).astype(BF)
    both = nt_dot(left, at_slot)
    goals = both[:OWN] * 16.0 + both[OWN:]
    for owner_id in range(OWN):
        table_ref[owner_id, 0:OWN, :] = table
        table_ref[owner_id, OWN : OWN + 8, :] = jnp.broadcast_to(
            goals[owner_id : owner_id + 1, :], (8, LIST)
        )
    rank_ref[...] = jnp.broadcast_to(rank, (8, ENT))


def gather_kernel(rows_ref, owner_ref, down_ref, hours_ref, send_ref, column_s):
    rows, keys = all_entries(rows_ref, owner_ref, down_ref)
    (rank,), _ = ranks([keys])
    fits = (keys > 0) & (rank < ONE)
    at_owner = (iota((OWN, ENT), 0) == ((keys - 1) >> 11)) & fits
    left = jnp.concatenate(
        [
            jnp.where(at_owner, (rows + 1) >> 4, 0).astype(F32),
            jnp.where(at_owner, (rows + 1) & 15, 0).astype(F32),
        ],
        axis=0,
    ).astype(BF)
    slot = jnp.where(fits, rank, -1)
    at_slot = jnp.where(iota((LIST, ENT), 0) == slot, 1.0, 0.0).astype(BF)
    both = nt_dot(left, at_slot)
    column_s[...] = row_columns(both[:OWN] * 16.0 + both[OWN:])
    send_ref[...] = pick_rows(column_s, ONE, hours_ref[0])


def plan_kernel(
    rows_ref,
    owner_ref,
    down_ref,
    rank_ref,
    full_ref,
    column_ref,
    hop_ref,
    goal_ref,
    left_ref,
    meta_ref,
    full_s,
):
    pltpu.sync_copy(full_ref, full_s)
    for owner in range(OWN):
        goal_ref[owner : owner + 1, :] = full_s[owner, OWN : OWN + 8, :][0:1]
    full = full_s[:, 0:OWN, :].reshape(OWN * OWN, LIST).astype(I32)
    parts = jnp.concatenate([(full >> 8).astype(F32), (full & 255).astype(F32)], axis=1)
    parts_t = jnp.transpose(parts).astype(BF)
    rows, first_keys = all_entries(rows_ref, owner_ref, down_ref)
    keys = [first_keys]
    for _ in range(1, HOPS):
        at = keys[-1] - 1
        pick_hi = jnp.where(iota((OWN * OWN, ENT), 0) == (at >> 7), 1.0, 0.0).astype(BF)
        found = nn_dot(parts_t, pick_hi)
        value = found[:LIST] * 256.0 + found[LIST:]
        at_lo = iota((LIST, ENT), 0) == (at & 127)
        keys.append(jnp.sum(jnp.where(at_lo, value, 0.0), axis=0, keepdims=True).astype(I32))
    order = list(range(HOPS - 1, -1, -1))
    first_fits = rank_ref[0:1, :] < ONE
    keys[0] = jnp.where(first_fits, 0, keys[0])
    found, listed = ranks([keys[hop] for hop in order])
    slots = [None] * HOPS
    rest = [None] * HOPS
    for place, hop in enumerate(order):
        limit = DEEP if hop >= 2 else DATA
        used = keys[hop] > 0
        slots[hop] = jnp.where(used & (found[place] < limit), found[place], -1)
        rest[hop] = jnp.where(used & (found[place] >= limit), keys[hop], 0)
    found, totals = ranks([rest[hop] for hop in order])
    most_left = jnp.max(totals, axis=0, keepdims=True)
    for place, hop in enumerate(order):
        left_ref[pl.ds(hop, 1), :] = jnp.where(rest[hop] > 0, found[place], -1)
        left_ref[pl.ds(8 + hop, 1), :] = rest[hop]
    meta = jnp.zeros((5 * OWN, LIST), F32)
    for hop in range(HOPS):
        at = keys[hop] - 1
        owner = at >> 11
        goal = (at & (SUBS - 1)) + 1
        at_owner = (iota((OWN, ENT), 0) == owner) & (slots[hop] >= 0)
        left = jnp.concatenate(
            [
                jnp.where(at_owner, goal >> 4, 0).astype(F32),
                jnp.where(at_owner, goal & 15, 0).astype(F32),
                jnp.where(at_owner, float(hop + 1), 0.0),
                jnp.where(at_owner, (rows + 1) >> 4, 0).astype(F32),
                jnp.where(at_owner, (rows + 1) & 15, 0).astype(F32),
            ],
            axis=0,
        ).astype(BF)
        right = jnp.where(iota((LIST, ENT), 0) == slots[hop], 1.0, 0.0).astype(BF)
        meta = meta + nt_dot(left, right)
    goals = meta[:OWN] * 16.0 + meta[OWN : 2 * OWN]
    scan = jnp.minimum(listed, float(DATA)) + 1.0
    meta_ref[:, 0:128] = jnp.where(iota((OWN, LIST), 1) == LIST - 1, scan, goals)
    meta_ref[:, 128:256] = jnp.zeros((OWN, 128), F32)
    hop_ref[...] = row_columns(meta[2 * OWN : 3 * OWN] + 1.0)
    column_ref[...] = row_columns(meta[3 * OWN : 4 * OWN] * 16.0 + meta[4 * OWN :])
    meta_ref[:, 256:384] = jnp.broadcast_to(most_left, (OWN, 128))
    meta_ref[:, 384:512] = jnp.zeros((OWN, 128), F32)


EXT_R = 144
EXT_C = 768


def fetch(sources, places, sems):
    copies = [
        pltpu.make_async_copy(src, dst, sems.at[k]) for k, (src, dst) in enumerate(zip(sources, places))
    ]
    for copy in copies:
        copy.start()
    for copy in copies:
        copy.wait()


def strip_kernel(
    d_ref, c_ref, r_ref, f_ref, north_any, south_any, west_ref, east_ref, north_ref, south_ref, sems
):
    fetch((north_any, south_any), (north_ref, south_ref), sems)
    lane = iota((ROWS, 128), 1)
    lane4 = iota((4, 128), 1)
    west_ref[...] = jnp.zeros((EXT_R, 128), F32)
    east_ref[...] = jnp.zeros((EXT_R, 128), F32)
    sides = ((west_ref, 0, 0), (east_ref, COLS - 128, 124))
    for out_ref, start, first in sides:
        body = jnp.zeros((ROWS, 128), F32)
        top = jnp.zeros((4, 128), F32)
        bottom = jnp.zeros((4, 128), F32)
        for index, ref in enumerate((d_ref, c_ref, r_ref, f_ref)):
            shift = (4 * index - first) % 128
            block = ref[:, start : start + 128]
            if index == 3:
                block = block.astype(F32)
            mine = (lane >= 4 * index) & (lane < 4 * index + 4)
            mine4 = (lane4 >= 4 * index) & (lane4 < 4 * index + 4)
            body = jnp.where(mine, roll(block, shift, 1), body)
            top = jnp.where(mine4, roll(north_ref[index, :, start : start + 128], shift, 1), top)
            bottom = jnp.where(mine4, roll(south_ref[index, :, start : start + 128], shift, 1), bottom)
        out_ref[8 : 8 + ROWS, :] = body
        out_ref[4:8, :] = top
        out_ref[8 + ROWS : 12 + ROWS, :] = bottom


def shift_lanes(x, places):
    blocks = x.shape[1] // 128
    turned = [roll(x[:, b * 128 : (b + 1) * 128], places, 1) for b in range(blocks)]
    lane = iota(turned[0].shape, 1)
    zero = jnp.zeros_like(turned[0])
    out = []
    for b in range(blocks):
        if places > 0:
            other = turned[b - 1] if b else zero
            out.append(jnp.where(lane < places, other, turned[b]))
        else:
            other = turned[b + 1] if b + 1 < blocks else zero
            out.append(jnp.where(lane >= 128 + places, other, turned[b]))
    return jnp.concatenate(out, axis=1)


def roll(x, shift, axis):
    if shift % x.shape[axis] == 0:
        return x
    return pltpu.roll(x, shift % x.shape[axis], axis)


def main_kernel(
    d_ref,
    c_ref,
    r_ref,
    f_ref,
    north_any,
    south_any,
    west_any,
    east_any,
    nitro_ref,
    hours_ref,
    rows_ref,
    owner_ref,
    down_ref,
    rank_ref,
    column_ref,
    hop_ref,
    meta_ref,
    water_out,
    nitro_out,
    excess_out,
    send_ref,
    w_s,
    c_s,
    r_s,
    f_s,
    o_s,
    n_s,
    u_s,
    t_s,
    north_ref,
    south_ref,
    west_ref,
    east_ref,
    sems,
):
    edges = (north_any, south_any, west_any, east_any)
    fetch(edges, (north_ref, south_ref, west_ref, east_ref), sems)
    lane = iota((EXT_R, 128), 1)
    for index, (src, dst) in enumerate(((d_ref, w_s), (c_ref, c_s), (r_ref, r_s), (f_ref, f_s))):
        dst[0:8, :] = jnp.zeros((8, EXT_C), F32)
        dst[136:144, :] = jnp.zeros((8, EXT_C), F32)
        body = src[...]
        if index == 3:
            body = body.astype(F32)
        dst[8:136, 128:640] = body
        dst[4:8, 128:640] = north_ref[index]
        dst[136:140, 128:640] = south_ref[index]
        left = roll(west_ref[...], 124 - 4 * index, 1)
        dst[:, 0:128] = jnp.where(lane >= 124, left, 0.0)
        right = roll(east_ref[...], -4 * index, 1)
        dst[:, 640:768] = jnp.where(lane < 4, right, 0.0)
    t_s[...] = jnp.zeros((ROWS, COLS), F32)
    n_s[...] = jnp.zeros((EXT_R + 16, EXT_C), F32)
    u_s[...] = jnp.zeros((EXT_R + 16, EXT_C), F32)
    for _ in range(STEPS):

        def first(chunk, carry):
            at = pl.multiple_of(chunk * 8, 8)
            water = w_s[pl.ds(at, 8), :]
            rate = c_s[pl.ds(at, 8), :] * jnp.exp(jnp.log(water * water) * (1.0 / 3.0))
            out = water * (1.0 - jnp.exp(-rate))
            code = f_s[pl.ds(at, 8), :]
            o_s[pl.ds(at, 8), :] = out
            n_s[pl.ds(at + 8, 8), :] = jnp.where(code == 2.0, out, 0.0)
            u_s[pl.ds(at + 8, 8), :] = jnp.where(code == 3.0, out, 0.0)
            return carry

        lax.fori_loop(0, EXT_R // 8, first, 0, unroll=2)

        for chunk in range(EXT_R // 8):
            at = chunk * 8
            out = o_s[at : at + 8, :]
            code = f_s[at : at + 8, :]
            from_west = shift_lanes(jnp.where(code == 0.0, out, 0.0), 1)
            from_east = shift_lanes(jnp.where(code == 1.0, out, 0.0), -1)
            from_north = n_s[at + 7 : at + 15, :]
            from_south = u_s[at + 9 : at + 17, :]
            total = from_west + from_east + from_north + from_south
            w_s[at : at + 8, :] = w_s[at : at + 8, :] - out + total + r_s[at : at + 8, :]
            if 1 <= chunk <= 16:
                t_s[at - 8 : at, :] = t_s[at - 8 : at, :] + out[:, 128:640]

    nitro_out[...] = nitro_ref[...] * jnp.exp(-WASH * t_s[...])
    water = w_s[8:136, 128:640]
    water_out[...] = water
    blocks = jnp.where(iota((32, COLS), 1) // SUB_COLS == iota((32, COLS), 0), 1.0, 0.0)
    by_row = lax.dot_general(
        blocks, water, (((1,), (1,)), ((), ())), precision=EXACT, preferred_element_type=F32
    )
    pairs = jnp.where(iota((ROWS, 128), 0) // SUB_ROWS == iota((ROWS, 128), 1), 1.0, 0.0)
    means = lax.dot_general(
        by_row, pairs, (((1,), (0,)), ((), ())), precision=EXACT, preferred_element_type=F32
    ) * (1.0 / (SUB_ROWS * SUB_COLS))
    for block in range(ROWS // SUB_ROWS):
        at = block * 32
        factor = jnp.broadcast_to(means[:, block : block + 1], (32, 128))
        factor = jnp.concatenate([factor] * (HRS // 128), axis=1)
        excess = hours_ref[0, at : at + 32, :].astype(F32) * factor
        excess_out[at : at + 32, :] = excess.astype(BF)
    rows, keys = all_entries(rows_ref, owner_ref, down_ref)
    at_block = jnp.where(iota((128, ENT), 0) == (rows >> 5), 1.0, 0.0)
    found = lax.dot_general(
        means, at_block, (((1,), (0,)), ((), ())), precision=EXACT, preferred_element_type=F32
    )
    at_cell = iota((32, ENT), 0) == (rows & 31)
    entry_yield = jnp.sum(jnp.where(at_cell, found, 0.0), axis=0, keepdims=True)
    rank = rank_ref[0:1, :]
    fits = (keys > 0) & (rank < ONE)
    at_owner = (iota((OWN, ENT), 0) == ((keys - 1) >> 11)) & fits
    at_slot = jnp.where(iota((LIST, ENT), 0) == jnp.where(fits, rank, -1), 1.0, 0.0)
    slot_yield = lax.dot_general(
        jnp.where(at_owner, entry_yield, 0.0),
        at_slot,
        (((1,), (1,)), ((), ())),
        precision=EXACT,
        preferred_element_type=F32,
    )
    picked = pick_rows(column_ref, TWO, excess_out[...])
    counts = []
    parts = []
    for owner in range(OWN):
        count = jnp.broadcast_to(hop_ref[0:TWO, owner : owner + 1], (TWO, 128))
        counts.append(jnp.concatenate([count] * (HRS // 128), axis=1))
        parts.append(jnp.where(counts[owner] > 1, lag(picked[owner]), picked[owner]))
    deep = jnp.concatenate([x[0:DEEP] for x in parts], axis=0)
    deep_counts = jnp.concatenate([x[0:DEEP] for x in counts], axis=0)
    for hop in range(2, HOPS):
        deep = jnp.where(deep_counts > hop, lag(deep), deep)
    for owner in range(OWN):
        send_ref[owner, 0:DEEP, :] = deep[owner * DEEP : (owner + 1) * DEEP]
        send_ref[owner, DEEP:, :] = parts[owner][DEEP:]
        send_ref[owner, DATA : DATA + 1, :] = meta_ref[owner : owner + 1, :]
        send_ref[owner, DATA : DATA + 1, 128:256] = slot_yield[owner : owner + 1, :]


def lag(x):
    return RECENT * shift_lanes(x, 1) + EARLIER * shift_lanes(x, 2)


TILE = 1024
TILES = SUBS // TILE


def flat_line(lines, width):
    lane = iota((8, 128), 1)
    store = [jnp.zeros((8, 128), F32)] * (OWN * width // 128)
    for src in range(OWN):
        start = src * width
        block, off = start // 128, start % 128
        here = (lane >= off) & (lane < off + width)
        store[block] = jnp.where(here, roll(lines[src], off, 1), store[block])
    return jnp.concatenate(store, axis=1).astype(I32) - 1


def columns_of(lines):
    padded = jnp.concatenate([x[0:1] for x in lines] + [jnp.zeros((128 - OWN, 128), F32)], axis=0)
    return jnp.transpose(padded)


def final_kernel(
    one_ref,
    two_ref,
    goal_ref,
    excess_ref,
    kernel_ref,
    out_ref,
    rounds_ref,
    rows_s,
    line_s,
    goal_s,
    sum_s,
    target_s,
):
    step = pl.program_id(0)

    @pl.when(step == 0)
    def _():
        groups = [two_ref[src, TWO - 8 : TWO, :][7:8] for src in range(OWN)]
        for src in range(OWN):
            line_s[src : src + 1, :] = groups[src][:, 0:128].astype(I32) - 1
        pltpu.sync_copy(line_s, target_s)
        sum_s[...] = jnp.zeros(sum_s.shape, F32)
        for src in range(OWN):

            def add_row(slot, carry):
                target = target_s[src, slot]
                target = jnp.where(target >= 0, target, SUBS)
                row = two_ref[src, pl.ds(slot, 1), :]
                sum_s[pl.ds(target, 1), :] = sum_s[pl.ds(target, 1), :] + row
                return carry

            lax.fori_loop(0, target_s[src, LIST - 1], add_row, 0)
        goal_s[...] = flat_line(
            [jnp.broadcast_to(goal_ref[src : src + 1, :], (8, 128)) for src in range(OWN)], ONE
        )
        most = groups[0][:, 256:384]
        for x in groups[1:]:
            most = jnp.maximum(most, x[:, 256:384])
        rounds_ref[0, 0] = jnp.max(most).astype(I32)
        factors = columns_of([x[:, 128:256] for x in groups])
        for src in range(OWN):
            factor = jnp.broadcast_to(factors[0:ONE, src : src + 1], (ONE, 128))
            factor = jnp.concatenate([factor] * (HRS // 128), axis=1)
            rows_s[src * ONE : (src + 1) * ONE, :] = (one_ref[src] * factor).astype(BF)

    match = iota((TILE, OWN * ONE), 0) + step * TILE == goal_s[0:1, :]
    put = jnp.where(match, 1.0, 0.0).astype(BF)
    arrived = sum_s[pl.ds(pl.multiple_of(step * TILE, TILE), TILE), :]
    total = excess_ref[...].astype(F32) + lag(nn_dot(put, rows_s[...]) + arrived)
    high = total.astype(BF)
    low = (total - high.astype(F32)).astype(BF)
    half = HRS // 2
    parts = jnp.concatenate([high, low], axis=0)
    both = nn_dot(parts[:, :half], kernel_ref[:half, :half])
    out_ref[:, :half] = both[:TILE] + both[TILE:]
    both = nn_dot(parts, kernel_ref[:, half:])
    out_ref[:, half:] = both[:TILE] + both[TILE:]


def neighbours(axis):
    size = lax.axis_size(axis)
    up = [(i, i + 1) for i in range(size - 1)]
    return up, [(j, i) for i, j in up]


def exchange(array):
    return lax.all_to_all(array, "wide", split_axis=0, concat_axis=0, tiled=True)


def exact_dot(left, right):
    return jnp.dot(left, right, precision=EXACT, preferred_element_type=F32)


def routed_local(
    depth_start,
    conveyance,
    cell_rain,
    nitrogen,
    flow_dir,
    unit_hydro,
    rain_hours,
    send_rows,
    send_owner,
    send_down,
):
    lists = (send_rows, send_owner, send_down)
    fields = (depth_start, conveyance, cell_rain, flow_dir)
    anywhere = pl.BlockSpec(memory_space=pl.ANY)
    whole = lambda shape: pl.BlockSpec(shape, lambda i: (0,) * len(shape))
    table, rank, last, initial = pl.pallas_call(
        front_kernel,
        grid=(1,),
        out_shape=[
            jax.ShapeDtypeStruct((OWN, TABLE, LIST), F32),
            jax.ShapeDtypeStruct((8, ENT), I32),
            jax.ShapeDtypeStruct((4, 4, COLS), F32),
            jax.ShapeDtypeStruct((4, 4, COLS), F32),
        ],
        in_specs=[whole((1, LEV, 1, LIST))] * 3
        + [pl.BlockSpec((8, COLS), lambda i: (0, 0))] * 4
        + [pl.BlockSpec((8, COLS), lambda i: (ROWS // 8 - 1, 0))] * 4,
        out_specs=[
            whole((OWN, TABLE, LIST)),
            whole((8, ENT)),
            whole((4, 4, COLS)),
            whole((4, 4, COLS)),
        ],
        name="front",
    )(*lists, *fields, *fields)
    full = exchange(table)
    up, down = neighbours("wide")
    north = lax.ppermute(last, "wide", up)
    south = lax.ppermute(initial, "wide", down)
    outgoing = pl.pallas_call(
        gather_kernel,
        out_shape=jax.ShapeDtypeStruct((OWN, ONE, HRS), F32),
        grid=(1,),
        in_specs=[whole(x.shape) for x in (*lists, rain_hours)],
        out_specs=whole((OWN, ONE, HRS)),
        scratch_shapes=[pltpu.VMEM((LIST, LIST), I32)],
        compiler_params=ROOM,
        name="gather_rain",
    )(*lists, rain_hours)
    arrived = exchange(outgoing)
    west_strip, east_strip = pl.pallas_call(
        strip_kernel,
        out_shape=[jax.ShapeDtypeStruct((EXT_R, 128), F32)] * 2,
        grid=(1,),
        in_specs=[whole(x.shape) for x in fields] + [anywhere] * 2,
        out_specs=[whole((EXT_R, 128))] * 2,
        scratch_shapes=[pltpu.VMEM((4, 4, COLS), F32)] * 2 + [pltpu.SemaphoreType.DMA((2,))],
        compiler_params=ROOM,
        name="strips",
    )(*fields, north, south)
    up, down = neighbours("narrow")
    west = lax.ppermute(east_strip, "narrow", up)
    east = lax.ppermute(west_strip, "narrow", down)
    columns, hops, goals, left, meta = pl.pallas_call(
        plan_kernel,
        out_shape=[
            jax.ShapeDtypeStruct((LIST, LIST), I32),
            jax.ShapeDtypeStruct((LIST, LIST), I32),
            jax.ShapeDtypeStruct((OWN, LIST), F32),
            jax.ShapeDtypeStruct((16, ENT), I32),
            jax.ShapeDtypeStruct((OWN, HRS), F32),
        ],
        grid=(1,),
        in_specs=[whole(x.shape) for x in (*lists, rank)] + [pl.BlockSpec(memory_space=pl.ANY)],
        out_specs=[
            whole((LIST, LIST)),
            whole((LIST, LIST)),
            whole((OWN, LIST)),
            whole((16, ENT)),
            whole((OWN, HRS)),
        ],
        scratch_shapes=[pltpu.VMEM((OWN, TABLE, LIST), F32)],
        compiler_params=ROOM,
        name="plan",
    )(*lists, rank, full)
    kernel = unit_hydro.astype(BF)
    pattern = jnp.concatenate([kernel, jnp.zeros((HRS,), BF)])
    repeated = jnp.tile(pattern, HRS)[: HRS * (2 * HRS - 1)]
    toeplitz = repeated.reshape(HRS, 2 * HRS - 1)[:, :HRS]
    flow_inputs = (*fields, north, south, west, east, nitrogen, rain_hours)
    flow_inputs += (*lists, rank, columns, hops, meta)
    water, nitrogen_left, excess, outgoing = pl.pallas_call(
        main_kernel,
        out_shape=[
            jax.ShapeDtypeStruct((ROWS, COLS), F32),
            jax.ShapeDtypeStruct((ROWS, COLS), F32),
            jax.ShapeDtypeStruct((SUBS, HRS), BF),
            jax.ShapeDtypeStruct((OWN, TWO, HRS), F32),
        ],
        grid=(1,),
        in_specs=[anywhere if 4 <= k < 8 else whole(x.shape) for k, x in enumerate(flow_inputs)],
        out_specs=[
            whole((ROWS, COLS)),
            whole((ROWS, COLS)),
            whole((SUBS, HRS)),
            whole((OWN, TWO, HRS)),
        ],
        scratch_shapes=[pltpu.VMEM((EXT_R, EXT_C), F32)] * 5
        + [pltpu.VMEM((EXT_R + 16, EXT_C), F32)] * 2
        + [pltpu.VMEM((ROWS, COLS), F32)]
        + [pltpu.VMEM((4, 4, COLS), F32)] * 2
        + [pltpu.VMEM((EXT_R, 128), F32)] * 2
        + [pltpu.SemaphoreType.DMA((4,))],
        name="flow_and_send",
    )(*flow_inputs)
    incoming = exchange(outgoing)
    tile = lambda i: (i, 0)
    discharge, most_left = pl.pallas_call(
        final_kernel,
        out_shape=[
            jax.ShapeDtypeStruct((SUBS, HRS), F32),
            jax.ShapeDtypeStruct((1, 1), I32),
        ],
        grid=(TILES,),
        in_specs=[
            whole((OWN, ONE, HRS)),
            whole((OWN, TWO, HRS)),
            whole((OWN, LIST)),
            pl.BlockSpec((TILE, HRS), tile),
            whole((HRS, HRS)),
        ],
        out_specs=[
            pl.BlockSpec((TILE, HRS), tile),
            pl.BlockSpec((1, 1), lambda i: (0, 0), memory_space=pltpu.SMEM),
        ],
        scratch_shapes=[
            pltpu.VMEM((OWN * ONE, HRS), BF),
            pltpu.VMEM((OWN, LIST), I32),
            pltpu.VMEM((8, OWN * ONE), I32),
            pltpu.VMEM((SUBS + 8, HRS), F32),
            pltpu.SMEM((OWN, LIST), I32),
        ],
        compiler_params=pltpu.CompilerParams(vmem_limit_bytes=50 << 20),
        name="route_and_convolve",
    )(arrived, incoming, goals, excess, toeplitz)

    def more(state):
        return state[0] * EXTRA < most_left[0, 0]

    def extra_round(state):
        index, flows = state
        valid = (send_rows >= 0) & (send_owner >= 0) & (send_down >= 0)
        rows_column = jnp.where(valid, send_rows, -1).reshape(ENT, 1)
        picker = (rows_column == jnp.arange(SUBS, dtype=I32)[None, :]).astype(F32)
        rows = exact_dot(picker, excess.astype(F32))
        slot_iota = jnp.arange(OWN * EXTRA, dtype=I32)
        send = jnp.zeros((OWN * EXTRA, HRS), F32)
        goals = jnp.zeros((OWN * EXTRA,), F32)
        for hop in range(HOPS):
            key = left[8 + hop] - 1
            rank = left[hop] - index * EXTRA
            here = (left[hop] >= 0) & (rank >= 0) & (rank < EXTRA)
            slot = jnp.where(here, (key >> 11) * EXTRA + rank, -1)
            placer = (slot[None, :] == slot_iota[:, None]).astype(F32)
            send = send + exact_dot(placer, rows)
            goals = goals + jnp.sum(placer * ((key & (SUBS - 1)) + 1).astype(F32)[None, :], axis=1)
            rows = lagged(rows)
        came = exchange(send.reshape(OWN, EXTRA, HRS)).reshape(-1, HRS)
        came_goals = exchange(goals.reshape(OWN, EXTRA)).reshape(-1).astype(I32) - 1
        routed = exact_dot(lagged(came), toeplitz.astype(F32))
        receiver = (came_goals[None, :] == jnp.arange(SUBS, dtype=I32)[:, None]).astype(F32)
        return index + 1, flows + exact_dot(receiver, routed)

    discharge = lax.while_loop(more, extra_round, (jnp.zeros((), I32), discharge))[1]
    return (water, nitrogen_left, discharge[None])


def lagged(flows):
    one_back = jnp.pad(flows, ((0, 0), (1, 0)))[:, :-1]
    two_back = jnp.pad(flows, ((0, 0), (2, 0)))[:, :-2]
    return RECENT * one_back + EARLIER * two_back


def solution(mesh):
    placed = (
        P("wide", "narrow"),
        P("wide", "narrow"),
        P("wide", "narrow"),
        P("wide", "narrow"),
        P("wide", "narrow"),
        P(),
        P("narrow", "wide", None),
        P("narrow", None, "wide", None),
        P("narrow", None, "wide", None),
        P("narrow", None, "wide", None),
    )
    return jax.shard_map(
        routed_local,
        mesh=mesh,
        in_specs=placed,
        out_specs=(P("wide", "narrow"), P("wide", "narrow"), P("narrow", "wide", None)),
        check_vma=False,
    )
```

```python
import jax
import jax.numpy as jnp
from jax import lax
from jax.experimental import pallas as pl
from jax.experimental.pallas import tpu as pltpu
from jax.sharding import PartitionSpec as P

SUB_ROWS = 2
SUB_COLS = 16
STEPS = 4
WASH = 1.5
RECENT = 0.6
EARLIER = 0.3
EXACT = lax.Precision.HIGHEST

OWN = 16
LEV = 5
LIST = 128
SUBS = 2048
HRS = 512
ROWS = 128
COLS = 512
HOPS = LEV
ENT = LEV * LIST

ONE = 64
TWO = 32
DATA = TWO - 1
DEEP = 8
EXTRA = 32
TABLE = 24

F32 = jnp.float32
BF = jnp.bfloat16
I32 = jnp.int32

ROOM = pltpu.CompilerParams(vmem_limit_bytes=26 << 20)


def nt_dot(a, b):
    return lax.dot_general(a, b, (((1,), (1,)), ((), ())), preferred_element_type=F32)


def nn_dot(a, b):
    return lax.dot_general(a, b, (((1,), (0,)), ((), ())), preferred_element_type=F32)


def iota(shape, dim):
    return lax.broadcasted_iota(I32, shape, dim)


def entry_keys(rows_ref, owner_ref, down_ref, level):
    rows = rows_ref[0, level]
    owner = owner_ref[0, level]
    down = down_ref[0, level]
    valid = (rows >= 0) & (owner >= 0) & (down >= 0)
    return jnp.where(valid, rows, -1), jnp.where(valid, owner * SUBS + down + 1, 0)


def upper_triangle():
    return jnp.where(iota((LIST, LIST), 0) < iota((LIST, LIST), 1), 1.0, 0.0).astype(BF)


def ranks(key_list):
    blocks = []
    for keys in key_list:
        owner = (keys - 1) >> 11
        for level in range(LEV):
            part = owner[:, level * LIST : (level + 1) * LIST]
            blocks.append(jnp.where(iota((OWN, LIST), 0) == part, 1.0, 0.0))
    counts = nn_dot(jnp.concatenate(blocks, axis=0).astype(BF), upper_triangle())
    base = jnp.zeros((OWN, 1), F32)
    pieces = []
    for index, block in enumerate(blocks):
        count = counts[index * OWN : (index + 1) * OWN]
        pieces.append(jnp.sum(block * (count + base), axis=0, keepdims=True))
        base = base + jnp.sum(block, axis=1, keepdims=True)
    out = []
    for index in range(len(key_list)):
        out.append(jnp.concatenate(pieces[index * LEV : (index + 1) * LEV], axis=1).astype(I32))
    return out, base


def all_entries(rows_ref, owner_ref, down_ref):
    both = [entry_keys(rows_ref, owner_ref, down_ref, level) for level in range(LEV)]
    return tuple(jnp.concatenate([pair[k] for pair in both], axis=1) for k in range(2))


def row_columns(table):
    padded = jnp.concatenate([table, jnp.zeros((LIST - OWN, LIST), F32)], axis=0)
    return jnp.transpose(padded).astype(I32) - 1


def pick_rows(column_ref, width, source):
    picks = []
    for owner in range(OWN):
        row = jnp.broadcast_to(column_ref[0:width, owner : owner + 1], (width, 128))
        row = jnp.concatenate([row] * (SUBS // 128), axis=1)
        picks.append(jnp.where(row == iota((width, SUBS), 1), 1.0, 0.0).astype(BF))
    return nn_dot(jnp.concatenate(picks, axis=0), source).reshape(OWN, width, HRS)


def front_kernel(
    rows_ref,
    owner_ref,
    down_ref,
    d_top,
    c_top,
    r_top,
    f_top,
    d_end,
    c_end,
    r_end,
    f_end,
    table_ref,
    rank_ref,
    last_ref,
    initial_ref,
):
    for index, (top, end) in enumerate(
        ((d_top, d_end), (c_top, c_end), (r_top, r_end), (f_top, f_end))
    ):
        initial_ref[index] = top[0:4, :].astype(F32)
        last_ref[index] = end[4:8, :].astype(F32)
    rows, keys = all_entries(rows_ref, owner_ref, down_ref)
    at_hi = iota((OWN, ENT), 0) == (rows >> 7)
    at_lo = jnp.where(iota((LIST, ENT), 0) == (rows & 127), 1.0, 0.0).astype(BF)
    left = jnp.concatenate(
        [
            jnp.where(at_hi, keys >> 8, 0).astype(F32),
            jnp.where(at_hi, keys & 255, 0).astype(F32),
        ],
        axis=0,
    ).astype(BF)
    both = nt_dot(left, at_lo)
    table = both[:OWN] * 256.0 + both[OWN:]
    (rank,), _ = ranks([keys])
    fits = (keys > 0) & (rank < ONE)
    owner = (keys - 1) >> 11
    goal = ((keys - 1) & (SUBS - 1)) + 1
    at_owner = (iota((OWN, ENT), 0) == owner) & fits
    left = jnp.concatenate(
        [
            jnp.where(at_owner, goal >> 4, 0).astype(F32),
            jnp.where(at_owner, goal & 15, 0).astype(F32),
        ],
        axis=0,
    ).astype(BF)
    slot = jnp.where(fits, rank, -1)
    at_slot = jnp.where(iota((LIST, ENT), 0) == slot, 1.0, 0.0).astype(BF)
    both = nt_dot(left, at_slot)
    goals = both[:OWN] * 16.0 + both[OWN:]
    for owner_id in range(OWN):
        table_ref[owner_id, 0:OWN, :] = table
        table_ref[owner_id, OWN : OWN + 8, :] = jnp.broadcast_to(
            goals[owner_id : owner_id + 1, :], (8, LIST)
        )
    rank_ref[...] = jnp.broadcast_to(rank, (8, ENT))


def gather_kernel(rows_ref, owner_ref, down_ref, hours_ref, send_ref, column_s):
    rows, keys = all_entries(rows_ref, owner_ref, down_ref)
    (rank,), _ = ranks([keys])
    fits = (keys > 0) & (rank < ONE)
    at_owner = (iota((OWN, ENT), 0) == ((keys - 1) >> 11)) & fits
    left = jnp.concatenate(
        [
            jnp.where(at_owner, (rows + 1) >> 4, 0).astype(F32),
            jnp.where(at_owner, (rows + 1) & 15, 0).astype(F32),
        ],
        axis=0,
    ).astype(BF)
    slot = jnp.where(fits, rank, -1)
    at_slot = jnp.where(iota((LIST, ENT), 0) == slot, 1.0, 0.0).astype(BF)
    both = nt_dot(left, at_slot)
    column_s[...] = row_columns(both[:OWN] * 16.0 + both[OWN:])
    send_ref[...] = pick_rows(column_s, ONE, hours_ref[0])


def plan_kernel(
    rows_ref,
    owner_ref,
    down_ref,
    rank_ref,
    full_ref,
    column_ref,
    hop_ref,
    goal_ref,
    left_ref,
    meta_ref,
    full_s,
):
    pltpu.sync_copy(full_ref, full_s)
    for owner in range(OWN):
        goal_ref[owner : owner + 1, :] = full_s[owner, OWN : OWN + 8, :][0:1]
    full = full_s[:, 0:OWN, :].reshape(OWN * OWN, LIST).astype(I32)
    parts = jnp.concatenate([(full >> 8).astype(F32), (full & 255).astype(F32)], axis=1)
    parts_t = jnp.transpose(parts).astype(BF)
    rows, first_keys = all_entries(rows_ref, owner_ref, down_ref)
    keys = [first_keys]
    for _ in range(1, HOPS):
        at = keys[-1] - 1
        pick_hi = jnp.where(iota((OWN * OWN, ENT), 0) == (at >> 7), 1.0, 0.0).astype(BF)
        found = nn_dot(parts_t, pick_hi)
        value = found[:LIST] * 256.0 + found[LIST:]
        at_lo = iota((LIST, ENT), 0) == (at & 127)
        keys.append(jnp.sum(jnp.where(at_lo, value, 0.0), axis=0, keepdims=True).astype(I32))
    order = list(range(HOPS - 1, -1, -1))
    first_fits = rank_ref[0:1, :] < ONE
    keys[0] = jnp.where(first_fits, 0, keys[0])
    found, listed = ranks([keys[hop] for hop in order])
    slots = [None] * HOPS
    rest = [None] * HOPS
    for place, hop in enumerate(order):
        limit = DEEP if hop >= 2 else DATA
        used = keys[hop] > 0
        slots[hop] = jnp.where(used & (found[place] < limit), found[place], -1)
        rest[hop] = jnp.where(used & (found[place] >= limit), keys[hop], 0)
    found, totals = ranks([rest[hop] for hop in order])
    most_left = jnp.max(totals, axis=0, keepdims=True)
    for place, hop in enumerate(order):
        left_ref[pl.ds(hop, 1), :] = jnp.where(rest[hop] > 0, found[place], -1)
        left_ref[pl.ds(8 + hop, 1), :] = rest[hop]
    meta = jnp.zeros((5 * OWN, LIST), F32)
    for hop in range(HOPS):
        at = keys[hop] - 1
        owner = at >> 11
        goal = (at & (SUBS - 1)) + 1
        at_owner = (iota((OWN, ENT), 0) == owner) & (slots[hop] >= 0)
        left = jnp.concatenate(
            [
                jnp.where(at_owner, goal >> 4, 0).astype(F32),
                jnp.where(at_owner, goal & 15, 0).astype(F32),
                jnp.where(at_owner, float(hop + 1), 0.0),
                jnp.where(at_owner, (rows + 1) >> 4, 0).astype(F32),
                jnp.where(at_owner, (rows + 1) & 15, 0).astype(F32),
            ],
            axis=0,
        ).astype(BF)
        right = jnp.where(iota((LIST, ENT), 0) == slots[hop], 1.0, 0.0).astype(BF)
        meta = meta + nt_dot(left, right)
    goals = meta[:OWN] * 16.0 + meta[OWN : 2 * OWN]
    scan = jnp.minimum(listed, float(DATA)) + 1.0
    meta_ref[:, 0:128] = jnp.where(iota((OWN, LIST), 1) == LIST - 1, scan, goals)
    meta_ref[:, 128:256] = jnp.zeros((OWN, 128), F32)
    hop_ref[...] = row_columns(meta[2 * OWN : 3 * OWN] + 1.0)
    column_ref[...] = row_columns(meta[3 * OWN : 4 * OWN] * 16.0 + meta[4 * OWN :])
    meta_ref[:, 256:384] = jnp.broadcast_to(most_left, (OWN, 128))
    meta_ref[:, 384:512] = jnp.zeros((OWN, 128), F32)


EXT_R = 144
EXT_C = 768


def fetch(sources, places, sems):
    copies = [
        pltpu.make_async_copy(src, dst, sems.at[k]) for k, (src, dst) in enumerate(zip(sources, places))
    ]
    for copy in copies:
        copy.start()
    for copy in copies:
        copy.wait()


def strip_kernel(
    d_ref, c_ref, r_ref, f_ref, north_any, south_any, west_ref, east_ref, north_ref, south_ref, sems
):
    fetch((north_any, south_any), (north_ref, south_ref), sems)
    lane = iota((ROWS, 128), 1)
    lane4 = iota((4, 128), 1)
    west_ref[...] = jnp.zeros((EXT_R, 128), F32)
    east_ref[...] = jnp.zeros((EXT_R, 128), F32)
    sides = ((west_ref, 0, 0), (east_ref, COLS - 128, 124))
    for out_ref, start, first in sides:
        body = jnp.zeros((ROWS, 128), F32)
        top = jnp.zeros((4, 128), F32)
        bottom = jnp.zeros((4, 128), F32)
        for index, ref in enumerate((d_ref, c_ref, r_ref, f_ref)):
            shift = (4 * index - first) % 128
            block = ref[:, start : start + 128]
            if index == 3:
                block = block.astype(F32)
            mine = (lane >= 4 * index) & (lane < 4 * index + 4)
            mine4 = (lane4 >= 4 * index) & (lane4 < 4 * index + 4)
            body = jnp.where(mine, roll(block, shift, 1), body)
            top = jnp.where(mine4, roll(north_ref[index, :, start : start + 128], shift, 1), top)
            bottom = jnp.where(mine4, roll(south_ref[index, :, start : start + 128], shift, 1), bottom)
        out_ref[8 : 8 + ROWS, :] = body
        out_ref[4:8, :] = top
        out_ref[8 + ROWS : 12 + ROWS, :] = bottom


def shift_lanes(x, places):
    blocks = x.shape[1] // 128
    turned = [roll(x[:, b * 128 : (b + 1) * 128], places, 1) for b in range(blocks)]
    lane = iota(turned[0].shape, 1)
    zero = jnp.zeros_like(turned[0])
    out = []
    for b in range(blocks):
        if places > 0:
            other = turned[b - 1] if b else zero
            out.append(jnp.where(lane < places, other, turned[b]))
        else:
            other = turned[b + 1] if b + 1 < blocks else zero
            out.append(jnp.where(lane >= 128 + places, other, turned[b]))
    return jnp.concatenate(out, axis=1)


def roll(x, shift, axis):
    if shift % x.shape[axis] == 0:
        return x
    return pltpu.roll(x, shift % x.shape[axis], axis)


def main_kernel(
    d_ref,
    c_ref,
    r_ref,
    f_ref,
    north_any,
    south_any,
    west_any,
    east_any,
    nitro_ref,
    hours_ref,
    rows_ref,
    owner_ref,
    down_ref,
    rank_ref,
    column_ref,
    hop_ref,
    meta_ref,
    water_out,
    nitro_out,
    excess_out,
    send_ref,
    w_s,
    c_s,
    r_s,
    f_s,
    o_s,
    n_s,
    u_s,
    t_s,
    north_ref,
    south_ref,
    west_ref,
    east_ref,
    sems,
):
    edges = (north_any, south_any, west_any, east_any)
    fetch(edges, (north_ref, south_ref, west_ref, east_ref), sems)
    lane = iota((EXT_R, 128), 1)
    for index, (src, dst) in enumerate(((d_ref, w_s), (c_ref, c_s), (r_ref, r_s), (f_ref, f_s))):
        dst[0:8, :] = jnp.zeros((8, EXT_C), F32)
        dst[136:144, :] = jnp.zeros((8, EXT_C), F32)
        body = src[...]
        if index == 3:
            body = body.astype(F32)
        dst[8:136, 128:640] = body
        dst[4:8, 128:640] = north_ref[index]
        dst[136:140, 128:640] = south_ref[index]
        left = roll(west_ref[...], 124 - 4 * index, 1)
        dst[:, 0:128] = jnp.where(lane >= 124, left, 0.0)
        right = roll(east_ref[...], -4 * index, 1)
        dst[:, 640:768] = jnp.where(lane < 4, right, 0.0)
    t_s[...] = jnp.zeros((ROWS, COLS), F32)
    n_s[...] = jnp.zeros((EXT_R + 16, EXT_C), F32)
    u_s[...] = jnp.zeros((EXT_R + 16, EXT_C), F32)
    for _ in range(STEPS):

        def first(chunk, carry):
            at = pl.multiple_of(chunk * 8, 8)
            water = w_s[pl.ds(at, 8), :]
            rate = c_s[pl.ds(at, 8), :] * jnp.exp(jnp.log(water * water) * (1.0 / 3.0))
            out = water * (1.0 - jnp.exp(-rate))
            code = f_s[pl.ds(at, 8), :]
            o_s[pl.ds(at, 8), :] = out
            n_s[pl.ds(at + 8, 8), :] = jnp.where(code == 2.0, out, 0.0)
            u_s[pl.ds(at + 8, 8), :] = jnp.where(code == 3.0, out, 0.0)
            return carry

        lax.fori_loop(0, EXT_R // 8, first, 0, unroll=2)

        for chunk in range(EXT_R // 8):
            at = chunk * 8
            out = o_s[at : at + 8, :]
            code = f_s[at : at + 8, :]
            from_west = shift_lanes(jnp.where(code == 0.0, out, 0.0), 1)
            from_east = shift_lanes(jnp.where(code == 1.0, out, 0.0), -1)
            from_north = n_s[at + 7 : at + 15, :]
            from_south = u_s[at + 9 : at + 17, :]
            total = from_west + from_east + from_north + from_south
            w_s[at : at + 8, :] = w_s[at : at + 8, :] - out + total + r_s[at : at + 8, :]
            if 1 <= chunk <= 16:
                t_s[at - 8 : at, :] = t_s[at - 8 : at, :] + out[:, 128:640]

    nitro_out[...] = nitro_ref[...] * jnp.exp(-WASH * t_s[...])
    water = w_s[8:136, 128:640]
    water_out[...] = water
    blocks = jnp.where(iota((32, COLS), 1) // SUB_COLS == iota((32, COLS), 0), 1.0, 0.0)
    by_row = lax.dot_general(
        blocks, water, (((1,), (1,)), ((), ())), precision=EXACT, preferred_element_type=F32
    )
    pairs = jnp.where(iota((ROWS, 128), 0) // SUB_ROWS == iota((ROWS, 128), 1), 1.0, 0.0)
    means = lax.dot_general(
        by_row, pairs, (((1,), (0,)), ((), ())), precision=EXACT, preferred_element_type=F32
    ) * (1.0 / (SUB_ROWS * SUB_COLS))
    for block in range(ROWS // SUB_ROWS):
        at = block * 32
        factor = jnp.broadcast_to(means[:, block : block + 1], (32, 128))
        factor = jnp.concatenate([factor] * (HRS // 128), axis=1)
        excess = hours_ref[0, at : at + 32, :].astype(F32) * factor
        excess_out[at : at + 32, :] = excess.astype(BF)
    rows, keys = all_entries(rows_ref, owner_ref, down_ref)
    at_block = jnp.where(iota((128, ENT), 0) == (rows >> 5), 1.0, 0.0)
    found = lax.dot_general(
        means, at_block, (((1,), (0,)), ((), ())), precision=EXACT, preferred_element_type=F32
    )
    at_cell = iota((32, ENT), 0) == (rows & 31)
    entry_yield = jnp.sum(jnp.where(at_cell, found, 0.0), axis=0, keepdims=True)
    rank = rank_ref[0:1, :]
    fits = (keys > 0) & (rank < ONE)
    at_owner = (iota((OWN, ENT), 0) == ((keys - 1) >> 11)) & fits
    at_slot = jnp.where(iota((LIST, ENT), 0) == jnp.where(fits, rank, -1), 1.0, 0.0)
    slot_yield = lax.dot_general(
        jnp.where(at_owner, entry_yield, 0.0),
        at_slot,
        (((1,), (1,)), ((), ())),
        precision=EXACT,
        preferred_element_type=F32,
    )
    picked = pick_rows(column_ref, TWO, excess_out[...])
    counts = []
    parts = []
    for owner in range(OWN):
        count = jnp.broadcast_to(hop_ref[0:TWO, owner : owner + 1], (TWO, 128))
        counts.append(jnp.concatenate([count] * (HRS // 128), axis=1))
        parts.append(jnp.where(counts[owner] > 1, lag(picked[owner]), picked[owner]))
    deep = jnp.concatenate([x[0:DEEP] for x in parts], axis=0)
    deep_counts = jnp.concatenate([x[0:DEEP] for x in counts], axis=0)
    for hop in range(2, HOPS):
        deep = jnp.where(deep_counts > hop, lag(deep), deep)
    for owner in range(OWN):
        send_ref[owner, 0:DEEP, :] = deep[owner * DEEP : (owner + 1) * DEEP]
        send_ref[owner, DEEP:, :] = parts[owner][DEEP:]
        send_ref[owner, DATA : DATA + 1, :] = meta_ref[owner : owner + 1, :]
        send_ref[owner, DATA : DATA + 1, 128:256] = slot_yield[owner : owner + 1, :]


def lag(x):
    return RECENT * shift_lanes(x, 1) + EARLIER * shift_lanes(x, 2)


TILE = 1024
TILES = SUBS // TILE


def flat_line(lines, width):
    lane = iota((8, 128), 1)
    store = [jnp.zeros((8, 128), F32)] * (OWN * width // 128)
    for src in range(OWN):
        start = src * width
        block, off = start // 128, start % 128
        here = (lane >= off) & (lane < off + width)
        store[block] = jnp.where(here, roll(lines[src], off, 1), store[block])
    return jnp.concatenate(store, axis=1).astype(I32) - 1


def columns_of(lines):
    padded = jnp.concatenate([x[0:1] for x in lines] + [jnp.zeros((128 - OWN, 128), F32)], axis=0)
    return jnp.transpose(padded)


def final_kernel(
    one_ref,
    two_ref,
    goal_ref,
    excess_ref,
    kernel_ref,
    out_ref,
    rounds_ref,
    rows_s,
    line_s,
    goal_s,
    sum_s,
    target_s,
    sem,
):
    step = pl.program_id(0)

    @pl.when(step == 0)
    def _():
        groups = [two_ref[src, TWO - 8 : TWO, :][7:8] for src in range(OWN)]
        for src in range(OWN):
            line_s[src : src + 1, :] = groups[src][:, 0:128].astype(I32) - 1
        targets = pltpu.make_async_copy(line_s, target_s, sem)
        targets.start()
        sum_s[...] = jnp.zeros(sum_s.shape, F32)
        goal_s[...] = flat_line(
            [jnp.broadcast_to(goal_ref[src : src + 1, :], (8, 128)) for src in range(OWN)], ONE
        )
        most = groups[0][:, 256:384]
        for x in groups[1:]:
            most = jnp.maximum(most, x[:, 256:384])
        rounds_ref[0, 0] = jnp.max(most).astype(I32)
        factors = columns_of([x[:, 128:256] for x in groups])
        for src in range(OWN):
            factor = jnp.broadcast_to(factors[0:ONE, src : src + 1], (ONE, 128))
            factor = jnp.concatenate([factor] * (HRS // 128), axis=1)
            rows_s[src * ONE : (src + 1) * ONE, :] = (one_ref[src] * factor).astype(BF)
        targets.wait()
        for src in range(OWN):

            def add_row(slot, carry):
                target = target_s[src, slot]
                target = jnp.where(target >= 0, target, SUBS)
                row = two_ref[src, pl.ds(slot, 1), :]
                sum_s[pl.ds(target, 1), :] = sum_s[pl.ds(target, 1), :] + row
                return carry

            lax.fori_loop(0, target_s[src, LIST - 1], add_row, 0)

    match = iota((TILE, OWN * ONE), 0) + step * TILE == goal_s[0:1, :]
    put = jnp.where(match, 1.0, 0.0).astype(BF)
    arrived = sum_s[pl.ds(pl.multiple_of(step * TILE, TILE), TILE), :]
    total = excess_ref[...].astype(F32) + lag(nn_dot(put, rows_s[...]) + arrived)
    high = total.astype(BF)
    low = (total - high.astype(F32)).astype(BF)
    half = HRS // 2
    parts = jnp.concatenate([high, low], axis=0)
    both = nn_dot(parts[:, :half], kernel_ref[:half, :half])
    out_ref[:, :half] = both[:TILE] + both[TILE:]
    both = nn_dot(parts, kernel_ref[:, half:])
    out_ref[:, half:] = both[:TILE] + both[TILE:]


def neighbours(axis):
    size = lax.axis_size(axis)
    up = [(i, i + 1) for i in range(size - 1)]
    return up, [(j, i) for i, j in up]


def exchange(array):
    return lax.all_to_all(array, "wide", split_axis=0, concat_axis=0, tiled=True)


def exact_dot(left, right):
    return jnp.dot(left, right, precision=EXACT, preferred_element_type=F32)


def routed_local(
    depth_start,
    conveyance,
    cell_rain,
    nitrogen,
    flow_dir,
    unit_hydro,
    rain_hours,
    send_rows,
    send_owner,
    send_down,
):
    lists = (send_rows, send_owner, send_down)
    fields = (depth_start, conveyance, cell_rain, flow_dir)
    anywhere = pl.BlockSpec(memory_space=pl.ANY)
    whole = lambda shape: pl.BlockSpec(shape, lambda i: (0,) * len(shape))
    table, rank, last, initial = pl.pallas_call(
        front_kernel,
        grid=(1,),
        out_shape=[
            jax.ShapeDtypeStruct((OWN, TABLE, LIST), F32),
            jax.ShapeDtypeStruct((8, ENT), I32),
            jax.ShapeDtypeStruct((4, 4, COLS), F32),
            jax.ShapeDtypeStruct((4, 4, COLS), F32),
        ],
        in_specs=[whole((1, LEV, 1, LIST))] * 3
        + [pl.BlockSpec((8, COLS), lambda i: (0, 0))] * 4
        + [pl.BlockSpec((8, COLS), lambda i: (ROWS // 8 - 1, 0))] * 4,
        out_specs=[
            whole((OWN, TABLE, LIST)),
            whole((8, ENT)),
            whole((4, 4, COLS)),
            whole((4, 4, COLS)),
        ],
        name="front",
    )(*lists, *fields, *fields)
    full = exchange(table)
    up, down = neighbours("wide")
    north = lax.ppermute(last, "wide", up)
    south = lax.ppermute(initial, "wide", down)
    outgoing = pl.pallas_call(
        gather_kernel,
        out_shape=jax.ShapeDtypeStruct((OWN, ONE, HRS), F32),
        grid=(1,),
        in_specs=[whole(x.shape) for x in (*lists, rain_hours)],
        out_specs=whole((OWN, ONE, HRS)),
        scratch_shapes=[pltpu.VMEM((LIST, LIST), I32)],
        compiler_params=ROOM,
        name="gather_rain",
    )(*lists, rain_hours)
    arrived = exchange(outgoing)
    west_strip, east_strip = pl.pallas_call(
        strip_kernel,
        out_shape=[jax.ShapeDtypeStruct((EXT_R, 128), F32)] * 2,
        grid=(1,),
        in_specs=[whole(x.shape) for x in fields] + [anywhere] * 2,
        out_specs=[whole((EXT_R, 128))] * 2,
        scratch_shapes=[pltpu.VMEM((4, 4, COLS), F32)] * 2 + [pltpu.SemaphoreType.DMA((2,))],
        compiler_params=ROOM,
        name="strips",
    )(*fields, north, south)
    up, down = neighbours("narrow")
    west = lax.ppermute(east_strip, "narrow", up)
    east = lax.ppermute(west_strip, "narrow", down)
    columns, hops, goals, left, meta = pl.pallas_call(
        plan_kernel,
        out_shape=[
            jax.ShapeDtypeStruct((LIST, LIST), I32),
            jax.ShapeDtypeStruct((LIST, LIST), I32),
            jax.ShapeDtypeStruct((OWN, LIST), F32),
            jax.ShapeDtypeStruct((16, ENT), I32),
            jax.ShapeDtypeStruct((OWN, HRS), F32),
        ],
        grid=(1,),
        in_specs=[whole(x.shape) for x in (*lists, rank)] + [pl.BlockSpec(memory_space=pl.ANY)],
        out_specs=[
            whole((LIST, LIST)),
            whole((LIST, LIST)),
            whole((OWN, LIST)),
            whole((16, ENT)),
            whole((OWN, HRS)),
        ],
        scratch_shapes=[pltpu.VMEM((OWN, TABLE, LIST), F32)],
        compiler_params=ROOM,
        name="plan",
    )(*lists, rank, full)
    kernel = unit_hydro.astype(BF)
    pattern = jnp.concatenate([kernel, jnp.zeros((HRS,), BF)])
    repeated = jnp.tile(pattern, HRS)[: HRS * (2 * HRS - 1)]
    toeplitz = repeated.reshape(HRS, 2 * HRS - 1)[:, :HRS]
    flow_inputs = (*fields, north, south, west, east, nitrogen, rain_hours)
    flow_inputs += (*lists, rank, columns, hops, meta)
    water, nitrogen_left, excess, outgoing = pl.pallas_call(
        main_kernel,
        out_shape=[
            jax.ShapeDtypeStruct((ROWS, COLS), F32),
            jax.ShapeDtypeStruct((ROWS, COLS), F32),
            jax.ShapeDtypeStruct((SUBS, HRS), BF),
            jax.ShapeDtypeStruct((OWN, TWO, HRS), F32),
        ],
        grid=(1,),
        in_specs=[anywhere if 4 <= k < 8 else whole(x.shape) for k, x in enumerate(flow_inputs)],
        out_specs=[
            whole((ROWS, COLS)),
            whole((ROWS, COLS)),
            whole((SUBS, HRS)),
            whole((OWN, TWO, HRS)),
        ],
        scratch_shapes=[pltpu.VMEM((EXT_R, EXT_C), F32)] * 5
        + [pltpu.VMEM((EXT_R + 16, EXT_C), F32)] * 2
        + [pltpu.VMEM((ROWS, COLS), F32)]
        + [pltpu.VMEM((4, 4, COLS), F32)] * 2
        + [pltpu.VMEM((EXT_R, 128), F32)] * 2
        + [pltpu.SemaphoreType.DMA((4,))],
        name="flow_and_send",
    )(*flow_inputs)
    incoming = exchange(outgoing)
    tile = lambda i: (i, 0)
    discharge, most_left = pl.pallas_call(
        final_kernel,
        out_shape=[
            jax.ShapeDtypeStruct((SUBS, HRS), F32),
            jax.ShapeDtypeStruct((1, 1), I32),
        ],
        grid=(TILES,),
        in_specs=[
            whole((OWN, ONE, HRS)),
            whole((OWN, TWO, HRS)),
            whole((OWN, LIST)),
            pl.BlockSpec((TILE, HRS), tile),
            whole((HRS, HRS)),
        ],
        out_specs=[
            pl.BlockSpec((TILE, HRS), tile),
            pl.BlockSpec((1, 1), lambda i: (0, 0), memory_space=pltpu.SMEM),
        ],
        scratch_shapes=[
            pltpu.VMEM((OWN * ONE, HRS), BF),
            pltpu.VMEM((OWN, LIST), I32),
            pltpu.VMEM((8, OWN * ONE), I32),
            pltpu.VMEM((SUBS + 8, HRS), F32),
            pltpu.SMEM((OWN, LIST), I32),
            pltpu.SemaphoreType.DMA,
        ],
        compiler_params=pltpu.CompilerParams(vmem_limit_bytes=50 << 20),
        name="route_and_convolve",
    )(arrived, incoming, goals, excess, toeplitz)

    def more(state):
        return state[0] * EXTRA < most_left[0, 0]

    def extra_round(state):
        index, flows = state
        valid = (send_rows >= 0) & (send_owner >= 0) & (send_down >= 0)
        rows_column = jnp.where(valid, send_rows, -1).reshape(ENT, 1)
        picker = (rows_column == jnp.arange(SUBS, dtype=I32)[None, :]).astype(F32)
        rows = exact_dot(picker, excess.astype(F32))
        slot_iota = jnp.arange(OWN * EXTRA, dtype=I32)
        send = jnp.zeros((OWN * EXTRA, HRS), F32)
        goals = jnp.zeros((OWN * EXTRA,), F32)
        for hop in range(HOPS):
            key = left[8 + hop] - 1
            rank = left[hop] - index * EXTRA
            here = (left[hop] >= 0) & (rank >= 0) & (rank < EXTRA)
            slot = jnp.where(here, (key >> 11) * EXTRA + rank, -1)
            placer = (slot[None, :] == slot_iota[:, None]).astype(F32)
            send = send + exact_dot(placer, rows)
            goals = goals + jnp.sum(placer * ((key & (SUBS - 1)) + 1).astype(F32)[None, :], axis=1)
            rows = lagged(rows)
        came = exchange(send.reshape(OWN, EXTRA, HRS)).reshape(-1, HRS)
        came_goals = exchange(goals.reshape(OWN, EXTRA)).reshape(-1).astype(I32) - 1
        routed = exact_dot(lagged(came), toeplitz.astype(F32))
        receiver = (came_goals[None, :] == jnp.arange(SUBS, dtype=I32)[:, None]).astype(F32)
        return index + 1, flows + exact_dot(receiver, routed)

    discharge = lax.while_loop(more, extra_round, (jnp.zeros((), I32), discharge))[1]
    return (water, nitrogen_left, discharge[None])


def lagged(flows):
    one_back = jnp.pad(flows, ((0, 0), (1, 0)))[:, :-1]
    two_back = jnp.pad(flows, ((0, 0), (2, 0)))[:, :-2]
    return RECENT * one_back + EARLIER * two_back


def solution(mesh):
    placed = (
        P("wide", "narrow"),
        P("wide", "narrow"),
        P("wide", "narrow"),
        P("wide", "narrow"),
        P("wide", "narrow"),
        P(),
        P("narrow", "wide", None),
        P("narrow", None, "wide", None),
        P("narrow", None, "wide", None),
        P("narrow", None, "wide", None),
    )
    return jax.shard_map(
        routed_local,
        mesh=mesh,
        in_specs=placed,
        out_specs=(P("wide", "narrow"), P("wide", "narrow"), P("narrow", "wide", None)),
        check_vma=False,
    )
```
